128 devices in a mesh: blk: 16 (over y_lo, x, core), mp: 8 (over z, y_hi).
Axes of the slice: x: 4, y: 4 (y_hi: 2, y_lo: 2; y = y_hi * 2 + y_lo), z: 4, core: 2. Of those that a mesh axis runs over, the one named last changes fastest.
Arguments:
- features: bfloat16 [32768, 768], P('blk', 'mp'), may hold values from -9 to 9
- edge_dst: int32 [1024], P('blk'), may hold values from 0 to 15
- edge_src: int32 [1024], P('blk'), may hold values from 0 to 255
- edge_mask: int32 [1024, 128, 128], P('blk'), may hold values 0 or 1
- gin_in: bfloat16 [768, 768], P(None, 'mp'), may hold values from -0.21875 to 0.21875
- gin_out: bfloat16 [768, 768], P('mp'), may hold values from -0.21875 to 0.21875
- w_query: bfloat16 [768, 512], P(None, 'mp'), may hold values from -1 to 1
- w_key: bfloat16 [768, 512], P(None, 'mp'), may hold values from -1 to 1
- w_value: bfloat16 [768, 512], P(None, 'mp'), may hold values from -0.21875 to 0.21875
- w_attn_out: bfloat16 [512, 768], P('mp'), may hold values from -4 to 4
- ffn_in: bfloat16 [768, 1536], P(None, 'mp'), may hold values from -0.21875 to 0.21875
- ffn_out: bfloat16 [1536, 768], P('mp'), may hold values from -0.15625 to 0.15625
Outputs:
- layer_out: bfloat16 [32768, 768], P('blk', 'mp')
The draws below stay inside these ranges and needn't reach their ends.
Inputs may be any that keep to these rules, and one draw needn't show every extreme that they name: `edge_dst`: local destination block of an edge block. `edge_src`: source block over the whole batch; several edge blocks may share a pair.
All inputs are finite; a program needn't handle non-finite values. No bound on the sum of `edge_mask` on one device may be relied on, other than what follows from the above.
Results may differ from the reference program's by a relative error of at most 0.011.
Values may be sent and summed in bfloat16 or wider, within the bound.
A program may use at most 128 MiB of HBM per device.

```python
import math
import jax
import jax.numpy as jnp
from jax import lax

D = 768
HEADS = 8
HEAD_DIM = 64
FF = 1536
BLOCK = 128
NODE_DEV = 2048
EB_DEV = 64
NODES = 32768
EDGES = 1024


def draw_features(key, part):
    base = jnp.clip(jax.random.normal(key, (NODES, D), jnp.float32), -4.0, 4.0)
    return base.astype(jnp.bfloat16)


def query_key_pair(key):
    seeded = jax.random.fold_in(key, 11)
    first = jnp.clip(jax.random.normal(jax.random.fold_in(seeded, 1), (D, HEADS * HEAD_DIM), jnp.float32), -4.0, 4.0)
    second = jnp.clip(jax.random.normal(jax.random.fold_in(seeded, 2), (D, HEADS * HEAD_DIM), jnp.float32), -4.0, 4.0)
    query = 2.0 * first / math.sqrt(D)
    keyed = second / math.sqrt(D)
    return (query, keyed)


def draw_w_query(key, part):
    return query_key_pair(key)[0].astype(jnp.bfloat16)


def draw_w_key(key, part):
    return query_key_pair(key)[1].astype(jnp.bfloat16)


def with_ends(drawn, key, smallest, high):
    longest = drawn.shape.index(max(drawn.shape))
    spots = []
    for shift in (0, 1):
        where = [jax.random.randint(jax.random.fold_in(key, axis), (), 0, length) for axis, length in enumerate(drawn.shape)]
        where[longest] = (where[longest] + shift) % drawn.shape[longest]
        spots.append(tuple(where))
    return drawn.at[spots[0]].set(smallest).at[spots[1]].set(high)


def levels(key, dims, pieces, low, top_value):
    gain = 1.0
    for axis_at, parts in pieces:
        draws = jax.random.uniform(jax.random.fold_in(jax.random.fold_in(key, 6), axis_at), (parts,), jnp.float32, low / len(pieces), top_value / len(pieces))
        gain = gain * jnp.repeat(jnp.exp(draws), dims[axis_at] // parts).reshape((-1,) + (1,) * (len(dims) - 1 - axis_at))
    return gain


def bell_draw(rng, extent, deviation, limit, pieces=(), kind=jnp.bfloat16):
    entries = jax.random.normal(rng, extent, jnp.float32) * deviation
    if len(pieces) > 0:
        entries = levels(rng, extent, pieces, -0.22, 0.18) * entries
    return jnp.clip(entries, min=-limit, max=limit).astype(kind)


def setup_inputs(seed: int = 0) -> dict:
    arg_keys = jax.random.split(jax.random.key(seed), 13)
    features = draw_features(jax.random.fold_in(arg_keys[12], 71), 0)
    edge_dst = with_ends(jax.random.randint(arg_keys[1], (EDGES,), 0, NODE_DEV // BLOCK), jax.random.fold_in(arg_keys[1], 1), 0, (NODE_DEV // BLOCK) - 1).astype(jnp.int32)
    edge_src = with_ends(jax.random.randint(arg_keys[2], (EDGES,), 0, NODES // BLOCK), jax.random.fold_in(arg_keys[2], 1), 0, (NODES // BLOCK) - 1).astype(jnp.int32)
    edge_mask = with_ends((jax.random.randint(arg_keys[3], (EDGES, BLOCK, BLOCK), 0, 8) < 1).astype(jnp.int32), jax.random.fold_in(arg_keys[3], 1), 0, 1)
    gin_in = bell_draw(arg_keys[4], (D, D), D ** -0.5, 0.21875, ((1, 8),))
    gin_out = bell_draw(arg_keys[5], (D, D), D ** -0.5, 0.21875, ((0, 8),))
    w_query = draw_w_query(jax.random.fold_in(arg_keys[12], 71), 0)
    w_key = draw_w_key(jax.random.fold_in(arg_keys[12], 71), 0)
    w_value = bell_draw(arg_keys[8], (D, HEADS * HEAD_DIM), D ** -0.5, 0.21875, ((1, 8),))
    w_attn_out = bell_draw(arg_keys[9], (HEADS * HEAD_DIM, D), (max(1, HEADS * HEAD_DIM // 256)) ** -0.5, 4.0, ((0, 8),))
    ffn_in = bell_draw(arg_keys[10], (D, FF), D ** -0.5, 0.21875, ((1, 8),))
    ffn_out = bell_draw(arg_keys[11], (FF, D), FF ** -0.5, 0.15625, ((0, 8),))
    return dict(features=features, edge_dst=edge_dst, edge_src=edge_src, edge_mask=edge_mask, gin_in=gin_in, gin_out=gin_out, w_query=w_query, w_key=w_key, w_value=w_value, w_attn_out=w_attn_out, ffn_in=ffn_in, ffn_out=ffn_out)


def reference(features, edge_dst, edge_src, edge_mask, gin_in, gin_out, w_query, w_key, w_value, w_attn_out, ffn_in, ffn_out):
    blocks = features.reshape(NODES // BLOCK, BLOCK, D)

    def add_edge(index, running_total):
        index = jnp.asarray(index).astype(jnp.int32)
        source = edge_src[index].astype(jnp.int32)
        target = (index // EB_DEV * (NODE_DEV // BLOCK) + edge_dst[index]).astype(jnp.int32)
        piece = lax.dynamic_index_in_dim(blocks, source, 0, keepdims=False)
        term = jnp.dot(edge_mask[index].astype(jnp.bfloat16), piece, preferred_element_type=jnp.float32)
        before = lax.dynamic_index_in_dim(running_total, target, 0, keepdims=False)
        return lax.dynamic_update_index_in_dim(running_total, before + term, target, 0)
    gathered = lax.fori_loop(0, EDGES, add_edge, jnp.zeros((NODES // BLOCK, BLOCK, D), jnp.float32))
    local_in = (features.astype(jnp.float32) + gathered.reshape(NODES, D) * 0.25).astype(jnp.bfloat16)
    local_hidden = jax.nn.relu(jnp.dot(local_in, gin_in, preferred_element_type=jnp.float32)).astype(jnp.bfloat16)
    queries = jnp.dot(features, w_query, preferred_element_type=jnp.float32).astype(jnp.bfloat16)
    keys = jnp.dot(features, w_key, preferred_element_type=jnp.float32).astype(jnp.bfloat16)
    values = jnp.dot(features, w_value, preferred_element_type=jnp.float32).astype(jnp.bfloat16)
    query_heads = queries.reshape(NODES, HEADS, HEAD_DIM).transpose(1, 0, 2)
    key_heads = keys.reshape(NODES, HEADS, HEAD_DIM).transpose(1, 0, 2)
    value_heads = values.reshape(NODES, HEADS, HEAD_DIM).transpose(1, 0, 2)
    row_block_tile = math.gcd(NODES, 1024)
    scale = 1.0 / math.sqrt(HEAD_DIM)

    def one_head(operands):
        head_q, head_k, head_v = operands

        def one_block(query_rows):
            scores = jnp.dot(query_rows, head_k.T, preferred_element_type=jnp.float32) * scale
            top = lax.optimization_barrier(jnp.max(scores, axis=-1, keepdims=True))
            expo = jnp.exp(scores - top)
            summed = jnp.dot(expo.astype(jnp.bfloat16), head_v, preferred_element_type=jnp.float32)
            return (summed / lax.optimization_barrier(jnp.sum(expo, axis=-1, keepdims=True))).astype(jnp.bfloat16)
        result = lax.map(one_block, head_q.reshape(NODES // row_block_tile, row_block_tile, HEAD_DIM))
        return result.reshape(NODES, HEAD_DIM)
    attended = lax.map(one_head, (query_heads, key_heads, value_heads))
    attended = attended.transpose(1, 0, 2).reshape(NODES, HEADS * HEAD_DIM)
    mixed = features.astype(jnp.float32) + jnp.dot(local_hidden, gin_out, preferred_element_type=jnp.float32) + jnp.dot(attended, w_attn_out, preferred_element_type=jnp.float32)
    row_average = lax.optimization_barrier(jnp.mean(mixed, axis=1, keepdims=True))
    square_row = lax.optimization_barrier(jnp.mean(mixed * mixed, axis=1, keepdims=True))
    normed = ((mixed - row_average) * lax.rsqrt(square_row - row_average * row_average + 1e-05)).astype(jnp.bfloat16)
    ffn_hidden = jax.nn.relu(jnp.dot(normed, ffn_in, preferred_element_type=jnp.float32)).astype(jnp.bfloat16)
    return (mixed + jnp.dot(ffn_hidden, ffn_out, preferred_element_type=jnp.float32)).astype(jnp.bfloat16)
```

```python
import functools
import math

import jax
import jax.numpy as jnp
from jax import lax
from jax.experimental import pallas as pl
from jax.experimental.pallas import tpu as pltpu
from jax.sharding import PartitionSpec as P

HEAD_DIM = 64
BLOCK = 128
Q_TILE = 1024
K_TILE = 1024


def neighbour_sum(features, edge_dst, edge_src, edge_mask, all_features):
    rows, cols = features.shape
    local_blocks = rows // BLOCK
    count = all_features.shape[0] // BLOCK
    blocks = all_features.reshape(count, BLOCK, cols)
    pulled = jnp.take(blocks, jnp.clip(edge_src, 0, count - 1), axis=0)
    summand_terms = jnp.einsum(
        "ers,esf->erf",
        edge_mask.astype(jnp.bfloat16),
        pulled,
        preferred_element_type=jnp.float32,
    )
    target_nodes = (
        edge_dst[:, None] == jnp.arange(local_blocks, dtype=jnp.int32)[None, :]
    ).astype(jnp.float32)
    running_total = jnp.einsum(
        "cy,cla->yla", target_nodes, summand_terms, precision=lax.Precision.HIGHEST
    )
    return running_total.reshape(rows, cols)


def flash_kernel(q_ref, k_ref, v_ref, o_ref, m_ref, l_ref, acc_ref):
    j = pl.program_id(1)

    @pl.when(j == 0)
    def _():
        m_ref[...] = jnp.full(m_ref.shape, -jnp.inf, jnp.float32)
        l_ref[...] = jnp.zeros(l_ref.shape, jnp.float32)
        acc_ref[...] = jnp.zeros(acc_ref.shape, jnp.float32)

    s = lax.dot_general(
        q_ref[...], k_ref[...], (((1,), (1,)), ((), ())), preferred_element_type=jnp.float32
    )
    m_prev = m_ref[...]
    m_new = jnp.maximum(m_prev, jnp.max(s, axis=1, keepdims=True))
    alpha = jnp.exp(m_prev - m_new)
    p = jnp.exp(s - m_new)
    l_ref[...] = alpha * l_ref[...] + jnp.sum(p, axis=1, keepdims=True)
    acc_ref[...] = alpha * acc_ref[...] + jnp.dot(
        p.astype(jnp.bfloat16), v_ref[...], preferred_element_type=jnp.float32
    )
    m_ref[...] = m_new

    @pl.when(j == pl.num_programs(1) - 1)
    def _():
        o_ref[...] = (acc_ref[...] / l_ref[...]).astype(o_ref.dtype)


def flash_attention(q, k, v):
    rows, dim = q.shape
    keys_n = k.shape[0]
    tq = min(Q_TILE, rows)
    tk = min(K_TILE, keys_n)
    grid = (rows // tq, keys_n // tk)
    return pl.pallas_call(
        flash_kernel,
        grid=grid,
        in_specs=[
            pl.BlockSpec((tq, dim), lambda i, j: (i, 0)),
            pl.BlockSpec((tk, dim), lambda i, j: (j, 0)),
            pl.BlockSpec((tk, dim), lambda i, j: (j, 0)),
        ],
        out_specs=pl.BlockSpec((tq, dim), lambda i, j: (i, 0)),
        out_shape=jax.ShapeDtypeStruct((rows, dim), jnp.bfloat16),
        scratch_shapes=[
            pltpu.VMEM((tq, 1), jnp.float32),
            pltpu.VMEM((tq, 1), jnp.float32),
            pltpu.VMEM((tq, dim), jnp.float32),
        ],
        compiler_params=pltpu.CompilerParams(
            dimension_semantics=("arbitrary", "arbitrary")
        ),
        cost_estimate=pl.CostEstimate(
            flops=4 * rows * keys_n * dim,
            transcendentals=rows * keys_n,
            bytes_accessed=2 * (rows * dim * 2 + grid[0] * keys_n * dim * 2),
        ),
    )(q, k, v)


def per_device(
    features,
    edge_dst,
    edge_src,
    edge_mask,
    gin_in,
    gin_out,
    w_query,
    w_key,
    w_value,
    w_attn_out,
    ffn_in,
    ffn_out,
):
    rows, cols = features.shape
    n_mp = lax.axis_size("mp")
    width = cols * n_mp
    share = rows // n_mp
    me = lax.axis_index("mp")
    heads = w_query.shape[1] // HEAD_DIM
    scale = 1.0 / math.sqrt(HEAD_DIM)

    whole = lax.all_gather(features, "mp", axis=1, tiled=True)
    all_features = lax.all_gather(features, "blk", axis=0, tiled=True)
    gin_in_full = lax.all_gather(gin_in, "mp", axis=1, tiled=True)
    gin_out_full = lax.all_gather(gin_out, "mp", axis=0, tiled=True)
    w_attn_out_full = lax.all_gather(w_attn_out, "mp", axis=0, tiled=True)
    ffn_in_full = lax.all_gather(ffn_in, "mp", axis=1, tiled=True)
    ffn_out_full = lax.all_gather(ffn_out, "mp", axis=0, tiled=True)

    queries = jnp.dot(whole, w_query, preferred_element_type=jnp.float32).astype(jnp.bfloat16)
    keys = jnp.dot(whole, w_key, preferred_element_type=jnp.float32).astype(jnp.bfloat16)
    values = jnp.dot(whole, w_value, preferred_element_type=jnp.float32).astype(jnp.bfloat16)
    queries = queries * jnp.bfloat16(scale)
    keys_all = lax.all_gather(keys, "blk", axis=0, tiled=True)
    values_all = lax.all_gather(values, "blk", axis=0, tiled=True)

    gathered = neighbour_sum(features, edge_dst, edge_src, edge_mask, all_features)
    local_share = (features.astype(jnp.float32) + gathered * 0.25).astype(jnp.bfloat16)

    attended = jnp.concatenate(
        [
            flash_attention(
                queries[:, h * HEAD_DIM : (h + 1) * HEAD_DIM],
                keys_all[:, h * HEAD_DIM : (h + 1) * HEAD_DIM],
                values_all[:, h * HEAD_DIM : (h + 1) * HEAD_DIM],
            )
            for h in range(heads)
        ],
        axis=1,
    )

    local_in = lax.all_to_all(local_share, "mp", 0, 1, tiled=True)
    attended_rows = lax.all_to_all(attended, "mp", 0, 1, tiled=True)
    own_rows = lax.dynamic_slice_in_dim(whole, me * share, share, 0).astype(jnp.float32)

    local_hidden = jax.nn.relu(
        jnp.dot(local_in, gin_in_full, preferred_element_type=jnp.float32)
    ).astype(jnp.bfloat16)
    mixed = (
        own_rows
        + jnp.dot(local_hidden, gin_out_full, preferred_element_type=jnp.float32)
        + jnp.dot(attended_rows, w_attn_out_full, preferred_element_type=jnp.float32)
    )
    row_average = jnp.sum(mixed, axis=1, keepdims=True) / width
    square_row = jnp.sum(mixed * mixed, axis=1, keepdims=True) / width
    normed = (
        (mixed - row_average) * lax.rsqrt(square_row - row_average * row_average + 1e-05)
    ).astype(jnp.bfloat16)
    ffn_hidden = jax.nn.relu(
        jnp.dot(normed, ffn_in_full, preferred_element_type=jnp.float32)
    ).astype(jnp.bfloat16)
    out_rows = (
        mixed + jnp.dot(ffn_hidden, ffn_out_full, preferred_element_type=jnp.float32)
    ).astype(jnp.bfloat16)
    return lax.all_to_all(out_rows, "mp", 1, 0, tiled=True)


def solution(mesh):
    return jax.shard_map(
        per_device,
        mesh=mesh,
        in_specs=(
            P("blk", "mp"),
            P("blk"),
            P("blk"),
            P("blk", None, None),
            P(None, "mp"),
            P("mp", None),
            P(None, "mp"),
            P(None, "mp"),
            P(None, "mp"),
            P("mp", None),
            P(None, "mp"),
            P("mp", None),
        ),
        out_specs=P("blk", "mp"),
        check_vma=False,
    )
```

```python
import functools
import math

import jax
import jax.numpy as jnp
from jax import lax
from jax.experimental import pallas as pl
from jax.experimental.pallas import tpu as pltpu
from jax.sharding import PartitionSpec as P

HEAD_DIM = 64
BLOCK = 128
Q_TILE = 1024
K_TILE = 1024


def neighbour_sum(features, edge_dst, edge_src, edge_mask, all_features):
    rows, cols = features.shape
    local_blocks = rows // BLOCK
    count = all_features.shape[0] // BLOCK
    blocks = all_features.reshape(count, BLOCK, cols)
    pulled = jnp.take(blocks, jnp.clip(edge_src, 0, count - 1), axis=0)
    summand_terms = jnp.einsum(
        "ers,esf->erf",
        edge_mask.astype(jnp.bfloat16),
        pulled,
        preferred_element_type=jnp.float32,
    )
    target_nodes = (
        edge_dst[:, None] == jnp.arange(local_blocks, dtype=jnp.int32)[None, :]
    ).astype(jnp.float32)
    running_total = jnp.einsum(
        "cy,cla->yla", target_nodes, summand_terms, precision=lax.Precision.HIGHEST
    )
    return running_total.reshape(rows, cols)


def flash_kernel(dim, q_ref, kv_ref, o_ref, m_ref, l_ref, acc_ref):
    j = pl.program_id(1)

    @pl.when(j == 0)
    def _():
        m_ref[...] = jnp.full(m_ref.shape, -jnp.inf, jnp.float32)
        l_ref[...] = jnp.zeros(l_ref.shape, jnp.float32)
        acc_ref[...] = jnp.zeros(acc_ref.shape, jnp.float32)

    kv = kv_ref[...]
    s = lax.dot_general(
        q_ref[...], kv, (((1,), (1,)), ((), ())), preferred_element_type=jnp.float32
    )
    m_prev = m_ref[...]
    m_new = jnp.maximum(m_prev, jnp.max(s, axis=1, keepdims=True))
    alpha = jnp.exp(m_prev - m_new)
    p = jnp.exp(s - m_new)
    l_ref[...] = alpha * l_ref[...] + jnp.sum(p, axis=1, keepdims=True)
    acc_ref[...] = alpha * acc_ref[...] + jnp.dot(
        p.astype(jnp.bfloat16), kv, preferred_element_type=jnp.float32
    )
    m_ref[...] = m_new

    @pl.when(j == pl.num_programs(1) - 1)
    def _():
        o_ref[...] = (acc_ref[:, dim : 2 * dim] / l_ref[...]).astype(o_ref.dtype)


def flash_attention(q, packed_all, head, heads):
    rows, dim = q.shape
    keys_n = packed_all.shape[0]
    tq = min(Q_TILE, rows)
    tk = min(K_TILE, keys_n)
    grid = (rows // tq, keys_n // tk)
    assert heads == 1
    lanes = 2 * dim
    q_pad = jnp.concatenate([q, jnp.zeros((rows, lanes - dim), q.dtype)], axis=1)
    return pl.pallas_call(
        functools.partial(flash_kernel, dim),
        grid=grid,
        in_specs=[
            pl.BlockSpec((tq, lanes), lambda i, j: (i, 0)),
            pl.BlockSpec((tk, lanes), lambda i, j: (j, 0)),
        ],
        out_specs=pl.BlockSpec((tq, dim), lambda i, j: (i, 0)),
        out_shape=jax.ShapeDtypeStruct((rows, dim), jnp.bfloat16),
        scratch_shapes=[
            pltpu.VMEM((tq, 1), jnp.float32),
            pltpu.VMEM((tq, 1), jnp.float32),
            pltpu.VMEM((tq, lanes), jnp.float32),
        ],
        compiler_params=pltpu.CompilerParams(
            dimension_semantics=("arbitrary", "arbitrary")
        ),
        cost_estimate=pl.CostEstimate(
            flops=4 * rows * keys_n * lanes,
            transcendentals=rows * keys_n,
            bytes_accessed=rows * lanes * 2 + grid[0] * keys_n * lanes * 2 + rows * dim * 2,
        ),
    )(q_pad, packed_all)


def per_device(
    features,
    edge_dst,
    edge_src,
    edge_mask,
    gin_in,
    gin_out,
    w_query,
    w_key,
    w_value,
    w_attn_out,
    ffn_in,
    ffn_out,
):
    rows, cols = features.shape
    n_mp = lax.axis_size("mp")
    width = cols * n_mp
    share = rows // n_mp
    me = lax.axis_index("mp")
    heads = w_query.shape[1] // HEAD_DIM
    scale = 1.0 / math.sqrt(HEAD_DIM)

    pieces = (features, gin_in, ffn_in, gin_out, w_attn_out, ffn_out)
    flat = jnp.concatenate([x.reshape(-1) for x in pieces])
    flat_all = lax.all_gather(flat, "mp", axis=0, tiled=False)
    unpacked = []
    offset = 0
    for x in pieces:
        size = x.size
        unpacked.append(flat_all[:, offset : offset + size].reshape((n_mp,) + x.shape))
        offset += size
    feats_parts, gin_in_parts, ffn_in_parts, gin_out_parts, attn_out_parts, ffn_out_parts = unpacked

    def join_columns(parts):
        count, r, c = parts.shape
        return parts.transpose(1, 0, 2).reshape(r, count * c)

    def join_rows(parts):
        count, r, c = parts.shape
        return parts.reshape(count * r, c)

    whole = join_columns(feats_parts)
    gin_in_full = join_columns(gin_in_parts)
    ffn_in_full = join_columns(ffn_in_parts)
    gin_out_full = join_rows(gin_out_parts)
    w_attn_out_full = join_rows(attn_out_parts)
    ffn_out_full = join_rows(ffn_out_parts)

    queries = jnp.dot(whole, w_query, preferred_element_type=jnp.float32).astype(jnp.bfloat16)
    keys = jnp.dot(whole, w_key, preferred_element_type=jnp.float32).astype(jnp.bfloat16)
    values = jnp.dot(whole, w_value, preferred_element_type=jnp.float32).astype(jnp.bfloat16)
    queries = queries * jnp.bfloat16(scale)
    kv_width = 2 * HEAD_DIM * heads
    lane_pad = (-(kv_width + cols)) % 128
    packed = jnp.concatenate(
        [keys, values, features, jnp.zeros((rows, lane_pad), jnp.bfloat16)], axis=1
    )
    packed_all = lax.all_gather(packed, "blk", axis=0, tiled=True)
    all_features = packed_all[:, kv_width : kv_width + cols]

    gathered = neighbour_sum(features, edge_dst, edge_src, edge_mask, all_features)
    local_share = (features.astype(jnp.float32) + gathered * 0.25).astype(jnp.bfloat16)

    attended = jnp.concatenate(
        [
            flash_attention(
                queries[:, h * HEAD_DIM : (h + 1) * HEAD_DIM],
                packed_all,
                h,
                heads,
            )
            for h in range(heads)
        ],
        axis=1,
    )

    mixed_in = jnp.concatenate([local_share, attended], axis=1).reshape(n_mp, share, -1)
    received = lax.all_to_all(mixed_in, "mp", 0, 0, tiled=False)
    local_in = join_columns(received[:, :, :cols])
    attended_rows = join_columns(received[:, :, cols:])
    own_rows = lax.dynamic_slice_in_dim(whole, me * share, share, 0).astype(jnp.float32)

    local_hidden = jax.nn.relu(
        jnp.dot(local_in, gin_in_full, preferred_element_type=jnp.float32)
    ).astype(jnp.bfloat16)
    mixed = (
        own_rows
        + jnp.dot(local_hidden, gin_out_full, preferred_element_type=jnp.float32)
        + jnp.dot(attended_rows, w_attn_out_full, preferred_element_type=jnp.float32)
    )
    row_average = jnp.sum(mixed, axis=1, keepdims=True) / width
    square_row = jnp.sum(mixed * mixed, axis=1, keepdims=True) / width
    normed = (
        (mixed - row_average) * lax.rsqrt(square_row - row_average * row_average + 1e-05)
    ).astype(jnp.bfloat16)
    ffn_hidden = jax.nn.relu(
        jnp.dot(normed, ffn_in_full, preferred_element_type=jnp.float32)
    ).astype(jnp.bfloat16)
    out_rows = (
        mixed + jnp.dot(ffn_hidden, ffn_out_full, preferred_element_type=jnp.float32)
    ).astype(jnp.bfloat16)
    out_parts = out_rows.reshape(share, n_mp, cols).transpose(1, 0, 2)
    return lax.all_to_all(out_parts, "mp", 0, 0, tiled=False).reshape(rows, cols)


def solution(mesh):
    return jax.shard_map(
        per_device,
        mesh=mesh,
        in_specs=(
            P("blk", "mp"),
            P("blk"),
            P("blk"),
            P("blk", None, None),
            P(None, "mp"),
            P("mp", None),
            P(None, "mp"),
            P(None, "mp"),
            P(None, "mp"),
            P("mp", None),
            P(None, "mp"),
            P("mp", None),
        ),
        out_specs=P("blk", "mp"),
        check_vma=False,
    )
```

```python
import functools
import math

import jax
import jax.numpy as jnp
from jax import lax
from jax.experimental import pallas as pl
from jax.experimental.pallas import tpu as pltpu
from jax.sharding import PartitionSpec as P

HEAD_DIM = 64
BLOCK = 128
Q_TILE = 1024
K_TILE = 1024


def neighbour_sum(features, edge_dst, edge_src, edge_mask, all_features):
    rows, cols = features.shape
    local_blocks = rows // BLOCK
    count = all_features.shape[0] // BLOCK
    blocks = all_features.reshape(count, BLOCK, cols)
    pulled = jnp.take(blocks, jnp.clip(edge_src, 0, count - 1), axis=0)
    summand_terms = jnp.einsum(
        "ers,esf->erf",
        edge_mask.astype(jnp.bfloat16),
        pulled,
        preferred_element_type=jnp.float32,
    )
    target_nodes = (
        edge_dst[:, None] == jnp.arange(local_blocks, dtype=jnp.int32)[None, :]
    ).astype(jnp.float32)
    running_total = jnp.einsum(
        "cy,cla->yla", target_nodes, summand_terms, precision=lax.Precision.HIGHEST
    )
    return running_total.reshape(rows, cols)


def flash_kernel(dim, q_ref, kv_ref, o_ref, m_ref, l_ref, acc_ref):
    j = pl.program_id(1)

    @pl.when(j == 0)
    def _():
        m_ref[...] = jnp.full(m_ref.shape, -jnp.inf, jnp.float32)
        l_ref[...] = jnp.zeros(l_ref.shape, jnp.float32)
        acc_ref[...] = jnp.zeros(acc_ref.shape, jnp.float32)

    kv = kv_ref[...]
    s = lax.dot_general(
        q_ref[...], kv, (((1,), (1,)), ((), ())), preferred_element_type=jnp.float32
    )
    m_prev = m_ref[...]
    m_new = jnp.maximum(m_prev, jnp.max(s, axis=1, keepdims=True))
    alpha = jnp.exp(m_prev - m_new)
    p = jnp.exp(s - m_new)
    l_ref[...] = alpha * l_ref[...] + jnp.sum(p, axis=1, keepdims=True)
    acc_ref[...] = alpha * acc_ref[...] + jnp.dot(
        p.astype(jnp.bfloat16), kv, preferred_element_type=jnp.float32
    )
    m_ref[...] = m_new

    @pl.when(j == pl.num_programs(1) - 1)
    def _():
        o_ref[...] = (acc_ref[:, dim : 2 * dim] / l_ref[...]).astype(o_ref.dtype)


def flash_attention(q, packed_all, head, heads):
    rows, dim = q.shape
    keys_n = packed_all.shape[0]
    tq = min(Q_TILE, rows)
    tk = min(K_TILE, keys_n)
    grid = (rows // tq, keys_n // tk)
    assert heads == 1
    lanes = 2 * dim
    q_pad = jnp.concatenate([q, jnp.zeros((rows, lanes - dim), q.dtype)], axis=1)
    return pl.pallas_call(
        functools.partial(flash_kernel, dim),
        grid=grid,
        in_specs=[
            pl.BlockSpec((tq, lanes), lambda i, j: (i, 0)),
            pl.BlockSpec((tk, lanes), lambda i, j: (j, 0)),
        ],
        out_specs=pl.BlockSpec((tq, dim), lambda i, j: (i, 0)),
        out_shape=jax.ShapeDtypeStruct((rows, dim), jnp.bfloat16),
        scratch_shapes=[
            pltpu.VMEM((tq, 1), jnp.float32),
            pltpu.VMEM((tq, 1), jnp.float32),
            pltpu.VMEM((tq, lanes), jnp.float32),
        ],
        compiler_params=pltpu.CompilerParams(
            dimension_semantics=("arbitrary", "arbitrary")
        ),
        cost_estimate=pl.CostEstimate(
            flops=4 * rows * keys_n * lanes,
            transcendentals=rows * keys_n,
            bytes_accessed=rows * lanes * 2 + grid[0] * keys_n * lanes * 2 + rows * dim * 2,
        ),
    )(q_pad, packed_all)


def per_device(
    features,
    edge_dst,
    edge_src,
    edge_mask,
    gin_in,
    gin_out,
    w_query,
    w_key,
    w_value,
    w_attn_out,
    ffn_in,
    ffn_out,
):
    rows, cols = features.shape
    n_mp = lax.axis_size("mp")
    width = cols * n_mp
    share = rows // n_mp
    me = lax.axis_index("mp")
    heads = w_query.shape[1] // HEAD_DIM
    scale = 1.0 / math.sqrt(HEAD_DIM)

    whole = lax.all_gather(features, "mp", axis=1, tiled=True)
    queries = jnp.dot(whole, w_query, preferred_element_type=jnp.float32).astype(jnp.bfloat16)
    keys = jnp.dot(whole, w_key, preferred_element_type=jnp.float32).astype(jnp.bfloat16)
    values = jnp.dot(whole, w_value, preferred_element_type=jnp.float32).astype(jnp.bfloat16)
    queries = queries * jnp.bfloat16(scale)
    kv_all = lax.all_gather(jnp.concatenate([keys, values], axis=1), "blk", axis=0, tiled=True)
    pieces = (gin_in, ffn_in, gin_out, w_attn_out, ffn_out)
    flat = jnp.concatenate([x.reshape(-1) for x in pieces])
    kv_all, late_features, flat = lax.optimization_barrier((kv_all, features, flat))
    all_features = lax.all_gather(late_features, "blk", axis=0, tiled=True)
    flat_all = lax.all_gather(flat, "mp", axis=0, tiled=False)
    unpacked = []
    offset = 0
    for x in pieces:
        size = x.size
        unpacked.append(flat_all[:, offset : offset + size].reshape((n_mp,) + x.shape))
        offset += size
    gin_in_parts, ffn_in_parts, gin_out_parts, attn_out_parts, ffn_out_parts = unpacked

    def join_columns(parts):
        count, r, c = parts.shape
        return parts.transpose(1, 0, 2).reshape(r, count * c)

    gin_in_full = join_columns(gin_in_parts).reshape(n_mp, cols, width)
    ffn_in_full = join_columns(ffn_in_parts)
    gin_out_full = gin_out_parts.reshape(width, width)
    ffn_out_full = ffn_out_parts.reshape(-1, width)

    gathered = neighbour_sum(features, edge_dst, edge_src, edge_mask, all_features)
    local_share = (features.astype(jnp.float32) + gathered * 0.25).astype(jnp.bfloat16)

    attended = flash_attention(queries, kv_all, 0, heads)

    mixed_in = jnp.concatenate([local_share, attended], axis=1).reshape(n_mp, share, -1)
    received = lax.all_to_all(mixed_in, "mp", 0, 0, tiled=False)
    own_rows = lax.dynamic_slice_in_dim(whole, me * share, share, 0).astype(jnp.float32)

    local_hidden = jax.nn.relu(
        jnp.einsum("jrc,jcd->rd", received[:, :, :cols], gin_in_full, preferred_element_type=jnp.float32)
    ).astype(jnp.bfloat16)
    mixed = (
        own_rows
        + jnp.dot(local_hidden, gin_out_full, preferred_element_type=jnp.float32)
        + jnp.einsum("jrd,jde->re", received[:, :, cols:], attn_out_parts, preferred_element_type=jnp.float32)
    )
    row_average = jnp.sum(mixed, axis=1, keepdims=True) / width
    square_row = jnp.sum(mixed * mixed, axis=1, keepdims=True) / width
    normed = (
        (mixed - row_average) * lax.rsqrt(square_row - row_average * row_average + 1e-05)
    ).astype(jnp.bfloat16)
    ffn_hidden = jax.nn.relu(
        jnp.dot(normed, ffn_in_full, preferred_element_type=jnp.float32)
    ).astype(jnp.bfloat16)
    out_rows = (
        mixed + jnp.dot(ffn_hidden, ffn_out_full, preferred_element_type=jnp.float32)
    ).astype(jnp.bfloat16)
    out_parts = out_rows.reshape(share, n_mp, cols).transpose(1, 0, 2)
    return lax.all_to_all(out_parts, "mp", 0, 0, tiled=False).reshape(rows, cols)


def solution(mesh):
    return jax.shard_map(
        per_device,
        mesh=mesh,
        in_specs=(
            P("blk", "mp"),
            P("blk"),
            P("blk"),
            P("blk", None, None),
            P(None, "mp"),
            P("mp", None),
            P(None, "mp"),
            P(None, "mp"),
            P(None, "mp"),
            P("mp", None),
            P(None, "mp"),
            P("mp", None),
        ),
        out_specs=P("blk", "mp"),
        check_vma=False,
    )
```

```python
import functools
import math

import jax
import jax.numpy as jnp
from jax import lax
from jax.experimental import pallas as pl
from jax.experimental.pallas import tpu as pltpu
from jax.sharding import PartitionSpec as P

HEAD_DIM = 64
BLOCK = 128
Q_TILE = 512
K_TILE = 4096


def neighbour_sum(features, edge_dst, edge_src, edge_mask, all_features):
    rows, cols = features.shape
    local_blocks = rows // BLOCK
    count = all_features.shape[0] // BLOCK
    blocks = all_features.reshape(count, BLOCK, cols)
    pulled = jnp.take(blocks, jnp.clip(edge_src, 0, count - 1), axis=0)
    summand_terms = jnp.einsum(
        "ers,esf->erf",
        edge_mask.astype(jnp.bfloat16),
        pulled,
        preferred_element_type=jnp.float32,
    )
    target_nodes = (
        edge_dst[:, None] == jnp.arange(local_blocks, dtype=jnp.int32)[None, :]
    ).astype(jnp.float32)
    running_total = jnp.einsum(
        "cy,cla->yla", target_nodes, summand_terms, precision=lax.Precision.HIGHEST
    )
    return running_total.reshape(rows, cols)


def flash_kernel(dim, q_ref, kv_ref, o_ref, m_ref, l_ref, acc_ref):
    j = pl.program_id(1)

    @pl.when(j == 0)
    def _():
        m_ref[...] = jnp.full(m_ref.shape, -jnp.inf, jnp.float32)
        l_ref[...] = jnp.zeros(l_ref.shape, jnp.float32)
        acc_ref[...] = jnp.zeros(acc_ref.shape, jnp.float32)

    kv = kv_ref[...]
    s = lax.dot_general(
        q_ref[...], kv, (((1,), (1,)), ((), ())), preferred_element_type=jnp.float32
    )
    m_prev = m_ref[...]
    m_new = jnp.maximum(m_prev, jnp.max(s, axis=1, keepdims=True))
    alpha = jnp.exp(m_prev - m_new)
    p = jnp.exp(s - m_new)
    l_ref[...] = alpha * l_ref[...] + jnp.sum(p, axis=1, keepdims=True)
    acc_ref[...] = alpha * acc_ref[...] + jnp.dot(
        p.astype(jnp.bfloat16), kv, preferred_element_type=jnp.float32
    )
    m_ref[...] = m_new

    @pl.when(j == pl.num_programs(1) - 1)
    def _():
        o_ref[...] = (acc_ref[:, dim : 2 * dim] / l_ref[...]).astype(o_ref.dtype)


def flash_attention(q, packed_all, head, heads):
    rows, dim = q.shape
    keys_n = packed_all.shape[0]
    tq = min(Q_TILE, rows)
    tk = min(K_TILE, keys_n)
    grid = (rows // tq, keys_n // tk)
    assert heads == 1
    lanes = 2 * dim
    q_pad = jnp.concatenate([q, jnp.zeros((rows, lanes - dim), q.dtype)], axis=1)
    return pl.pallas_call(
        functools.partial(flash_kernel, dim),
        grid=grid,
        in_specs=[
            pl.BlockSpec((tq, lanes), lambda i, j: (i, 0)),
            pl.BlockSpec((tk, lanes), lambda i, j: (j, 0)),
        ],
        out_specs=pl.BlockSpec((tq, dim), lambda i, j: (i, 0)),
        out_shape=jax.ShapeDtypeStruct((rows, dim), jnp.bfloat16),
        scratch_shapes=[
            pltpu.VMEM((tq, 1), jnp.float32),
            pltpu.VMEM((tq, 1), jnp.float32),
            pltpu.VMEM((tq, lanes), jnp.float32),
        ],
        compiler_params=pltpu.CompilerParams(
            dimension_semantics=("arbitrary", "arbitrary")
        ),
        cost_estimate=pl.CostEstimate(
            flops=4 * rows * keys_n * lanes,
            transcendentals=rows * keys_n,
            bytes_accessed=rows * lanes * 2 + grid[0] * keys_n * lanes * 2 + rows * dim * 2,
        ),
    )(q_pad, packed_all)


def per_device(
    features,
    edge_dst,
    edge_src,
    edge_mask,
    gin_in,
    gin_out,
    w_query,
    w_key,
    w_value,
    w_attn_out,
    ffn_in,
    ffn_out,
):
    rows, cols = features.shape
    n_mp = lax.axis_size("mp")
    width = cols * n_mp
    share = rows // n_mp
    me = lax.axis_index("mp")
    heads = w_query.shape[1] // HEAD_DIM
    scale = 1.0 / math.sqrt(HEAD_DIM)

    whole = lax.all_gather(features, "mp", axis=1, tiled=True)
    queries = jnp.dot(whole, w_query, preferred_element_type=jnp.float32).astype(jnp.bfloat16)
    keys = jnp.dot(whole, w_key, preferred_element_type=jnp.float32).astype(jnp.bfloat16)
    values = jnp.dot(whole, w_value, preferred_element_type=jnp.float32).astype(jnp.bfloat16)
    queries = queries * jnp.bfloat16(scale)
    kv_all = lax.all_gather(jnp.concatenate([keys, values], axis=1), "blk", axis=0, tiled=True)
    pieces = (gin_in, ffn_in, gin_out, w_attn_out, ffn_out)
    flat = jnp.concatenate([x.reshape(-1) for x in pieces])
    kv_all, late_features, flat = lax.optimization_barrier((kv_all, features, flat))
    all_features = lax.all_gather(late_features, "blk", axis=0, tiled=True)
    flat_all = lax.all_gather(flat, "mp", axis=0, tiled=False)
    unpacked = []
    offset = 0
    for x in pieces:
        size = x.size
        unpacked.append(flat_all[:, offset : offset + size].reshape((n_mp,) + x.shape))
        offset += size
    gin_in_parts, ffn_in_parts, gin_out_parts, attn_out_parts, ffn_out_parts = unpacked

    def join_columns(parts):
        count, r, c = parts.shape
        return parts.transpose(1, 0, 2).reshape(r, count * c)

    gin_in_full = join_columns(gin_in_parts).reshape(n_mp, cols, width)
    ffn_in_full = join_columns(ffn_in_parts)
    gin_out_full = gin_out_parts.reshape(width, width)
    ffn_out_full = ffn_out_parts.reshape(-1, width)

    gathered = neighbour_sum(features, edge_dst, edge_src, edge_mask, all_features)
    local_share = (features.astype(jnp.float32) + gathered * 0.25).astype(jnp.bfloat16)

    attended = flash_attention(queries, kv_all, 0, heads)

    mixed_in = jnp.concatenate([local_share, attended], axis=1).reshape(n_mp, share, -1)
    received = lax.all_to_all(mixed_in, "mp", 0, 0, tiled=False)
    own_rows = lax.dynamic_slice_in_dim(whole, me * share, share, 0).astype(jnp.float32)

    local_hidden = jax.nn.relu(
        jnp.einsum("jrc,jcd->rd", received[:, :, :cols], gin_in_full, preferred_element_type=jnp.float32)
    ).astype(jnp.bfloat16)
    mixed = (
        own_rows
        + jnp.dot(local_hidden, gin_out_full, preferred_element_type=jnp.float32)
        + jnp.einsum("jrd,jde->re", received[:, :, cols:], attn_out_parts, preferred_element_type=jnp.float32)
    )
    row_average = jnp.sum(mixed, axis=1, keepdims=True) / width
    square_row = jnp.sum(mixed * mixed, axis=1, keepdims=True) / width
    normed = (
        (mixed - row_average) * lax.rsqrt(square_row - row_average * row_average + 1e-05)
    ).astype(jnp.bfloat16)
    ffn_hidden = jax.nn.relu(
        jnp.dot(normed, ffn_in_full, preferred_element_type=jnp.float32)
    ).astype(jnp.bfloat16)
    out_rows = (
        mixed + jnp.dot(ffn_hidden, ffn_out_full, preferred_element_type=jnp.float32)
    ).astype(jnp.bfloat16)
    out_parts = out_rows.reshape(share, n_mp, cols).transpose(1, 0, 2)
    return lax.all_to_all(out_parts, "mp", 0, 0, tiled=False).reshape(rows, cols)


def solution(mesh):
    return jax.shard_map(
        per_device,
        mesh=mesh,
        in_specs=(
            P("blk", "mp"),
            P("blk"),
            P("blk"),
            P("blk", None, None),
            P(None, "mp"),
            P("mp", None),
            P(None, "mp"),
            P(None, "mp"),
            P(None, "mp"),
            P("mp", None),
            P(None, "mp"),
            P("mp", None),
        ),
        out_specs=P("blk", "mp"),
        check_vma=False,
    )
```

```python
import functools
import math

import jax
import jax.numpy as jnp
from jax import lax
from jax.experimental import pallas as pl
from jax.experimental.pallas import tpu as pltpu
from jax.sharding import PartitionSpec as P

HEAD_DIM = 64
BLOCK = 128
Q_TILE = 512
K_TILE = 4096


def neighbour_sum(features, edge_dst, edge_src, edge_mask, all_features):
    rows, cols = features.shape
    local_blocks = rows // BLOCK
    count = all_features.shape[0] // BLOCK
    blocks = all_features.reshape(count, BLOCK, cols)
    pulled = jnp.take(blocks, jnp.clip(edge_src, 0, count - 1), axis=0)
    summand_terms = jnp.einsum(
        "ers,esf->erf",
        edge_mask.astype(jnp.bfloat16),
        pulled,
        preferred_element_type=jnp.float32,
    )
    target_nodes = (
        edge_dst[:, None] == jnp.arange(local_blocks, dtype=jnp.int32)[None, :]
    ).astype(jnp.float32)
    running_total = jnp.einsum(
        "cy,cla->yla", target_nodes, summand_terms, precision=lax.Precision.HIGHEST
    )
    return running_total.reshape(rows, cols)


def flash_kernel(dim, q_ref, kv_ref, o_ref, m_ref, l_ref, acc_ref):
    j = pl.program_id(1)

    @pl.when(j == 0)
    def _():
        m_ref[...] = jnp.full(m_ref.shape, -jnp.inf, jnp.float32)
        l_ref[...] = jnp.zeros(l_ref.shape, jnp.float32)
        acc_ref[...] = jnp.zeros(acc_ref.shape, jnp.float32)

    kv = kv_ref[...]
    s = lax.dot_general(
        q_ref[...], kv, (((1,), (1,)), ((), ())), preferred_element_type=jnp.float32
    )
    m_prev = m_ref[...]
    m_new = jnp.maximum(m_prev, jnp.max(s, axis=1, keepdims=True))
    alpha = jnp.exp(m_prev - m_new)
    p = jnp.exp(s - m_new)
    l_ref[...] = alpha * l_ref[...] + jnp.sum(p, axis=1, keepdims=True)
    acc_ref[...] = alpha * acc_ref[...] + jnp.dot(
        p.astype(jnp.bfloat16), kv, preferred_element_type=jnp.float32
    )
    m_ref[...] = m_new

    @pl.when(j == pl.num_programs(1) - 1)
    def _():
        o_ref[...] = (acc_ref[:, dim : 2 * dim] / l_ref[...]).astype(o_ref.dtype)


def flash_attention(q, packed_all, head, heads):
    rows, dim = q.shape
    keys_n = packed_all.shape[0]
    tq = min(Q_TILE, rows)
    tk = min(K_TILE, keys_n)
    grid = (rows // tq, keys_n // tk)
    assert heads == 1
    lanes = 2 * dim
    q_pad = jnp.concatenate([q, jnp.zeros((rows, lanes - dim), q.dtype)], axis=1)
    return pl.pallas_call(
        functools.partial(flash_kernel, dim),
        grid=grid,
        in_specs=[
            pl.BlockSpec((tq, lanes), lambda i, j: (i, 0)),
            pl.BlockSpec((tk, lanes), lambda i, j: (j, 0)),
        ],
        out_specs=pl.BlockSpec((tq, dim), lambda i, j: (i, 0)),
        out_shape=jax.ShapeDtypeStruct((rows, dim), jnp.bfloat16),
        scratch_shapes=[
            pltpu.VMEM((tq, 1), jnp.float32),
            pltpu.VMEM((tq, 1), jnp.float32),
            pltpu.VMEM((tq, lanes), jnp.float32),
        ],
        compiler_params=pltpu.CompilerParams(
            dimension_semantics=("arbitrary", "arbitrary")
        ),
        cost_estimate=pl.CostEstimate(
            flops=4 * rows * keys_n * lanes,
            transcendentals=rows * keys_n,
            bytes_accessed=rows * lanes * 2 + grid[0] * keys_n * lanes * 2 + rows * dim * 2,
        ),
    )(q_pad, packed_all)


def gather_kernel(axis, n, x_ref, out_ref, send_sem, recv_sem, local_sem):
    me = lax.axis_index(axis)
    mesh_id = pl.DeviceIdType.MESH
    barrier = pltpu.get_barrier_semaphore()
    for k in range(1, n):
        pl.semaphore_signal(
            barrier, inc=1, device_id={axis: lax.rem(me + k, n)}, device_id_type=mesh_id
        )
    pl.semaphore_wait(barrier, n - 1)
    local = pltpu.make_async_copy(x_ref, out_ref.at[me], local_sem)
    local.start()
    sends = []
    for k in range(1, n):
        copy = pltpu.make_async_remote_copy(
            src_ref=x_ref,
            dst_ref=out_ref.at[me],
            send_sem=send_sem.at[k],
            recv_sem=recv_sem.at[k],
            device_id={axis: lax.rem(me + k, n)},
            device_id_type=mesh_id,
        )
        copy.start()
        sends.append(copy)
    for k in range(1, n):
        source = lax.rem(me + n - k, n)
        arriving = pltpu.make_async_remote_copy(
            src_ref=x_ref,
            dst_ref=out_ref.at[source],
            send_sem=send_sem.at[k],
            recv_sem=recv_sem.at[k],
            device_id={axis: source},
            device_id_type=mesh_id,
        )
        arriving.wait_recv()
    for copy in sends:
        copy.wait_send()
    local.wait()


def dma_all_gather(x, axis, collective_id):
    n = lax.axis_size(axis)
    return pl.pallas_call(
        functools.partial(gather_kernel, axis, n),
        in_specs=[pl.BlockSpec(memory_space=pl.ANY)],
        out_specs=pl.BlockSpec(memory_space=pl.ANY),
        out_shape=jax.ShapeDtypeStruct((n,) + x.shape, x.dtype),
        scratch_shapes=[
            pltpu.SemaphoreType.DMA((n,)),
            pltpu.SemaphoreType.DMA((n,)),
            pltpu.SemaphoreType.DMA,
        ],
        compiler_params=pltpu.CompilerParams(collective_id=collective_id, has_side_effects=True),
    )(x)


def per_device(
    features,
    edge_dst,
    edge_src,
    edge_mask,
    gin_in,
    gin_out,
    w_query,
    w_key,
    w_value,
    w_attn_out,
    ffn_in,
    ffn_out,
):
    rows, cols = features.shape
    n_mp = lax.axis_size("mp")
    width = cols * n_mp
    share = rows // n_mp
    me = lax.axis_index("mp")
    heads = w_query.shape[1] // HEAD_DIM
    scale = 1.0 / math.sqrt(HEAD_DIM)

    whole = dma_all_gather(features, "mp", 0).transpose(1, 0, 2).reshape(rows, width)
    queries = jnp.dot(whole, w_query, preferred_element_type=jnp.float32).astype(jnp.bfloat16)
    keys = jnp.dot(whole, w_key, preferred_element_type=jnp.float32).astype(jnp.bfloat16)
    values = jnp.dot(whole, w_value, preferred_element_type=jnp.float32).astype(jnp.bfloat16)
    queries = queries * jnp.bfloat16(scale)
    kv_all = lax.all_gather(jnp.concatenate([keys, values], axis=1), "blk", axis=0, tiled=True)
    pieces = (gin_in, ffn_in, gin_out, w_attn_out, ffn_out)
    flat = jnp.concatenate([x.reshape(-1) for x in pieces])
    kv_all, late_features, flat = lax.optimization_barrier((kv_all, features, flat))
    all_features = lax.all_gather(late_features, "blk", axis=0, tiled=True)
    flat_all = lax.all_gather(flat, "mp", axis=0, tiled=False)
    unpacked = []
    offset = 0
    for x in pieces:
        size = x.size
        unpacked.append(flat_all[:, offset : offset + size].reshape((n_mp,) + x.shape))
        offset += size
    gin_in_parts, ffn_in_parts, gin_out_parts, attn_out_parts, ffn_out_parts = unpacked

    def join_columns(parts):
        count, r, c = parts.shape
        return parts.transpose(1, 0, 2).reshape(r, count * c)

    gin_in_full = join_columns(gin_in_parts).reshape(n_mp, cols, width)
    ffn_in_full = join_columns(ffn_in_parts)
    gin_out_full = gin_out_parts.reshape(width, width)
    ffn_out_full = ffn_out_parts.reshape(-1, width)

    gathered = neighbour_sum(features, edge_dst, edge_src, edge_mask, all_features)
    local_share = (features.astype(jnp.float32) + gathered * 0.25).astype(jnp.bfloat16)

    attended = flash_attention(queries, kv_all, 0, heads)

    mixed_in = jnp.concatenate([local_share, attended], axis=1).reshape(n_mp, share, -1)
    received = lax.all_to_all(mixed_in, "mp", 0, 0, tiled=False)
    own_rows = lax.dynamic_slice_in_dim(whole, me * share, share, 0).astype(jnp.float32)

    local_hidden = jax.nn.relu(
        jnp.einsum("jrc,jcd->rd", received[:, :, :cols], gin_in_full, preferred_element_type=jnp.float32)
    ).astype(jnp.bfloat16)
    mixed = (
        own_rows
        + jnp.dot(local_hidden, gin_out_full, preferred_element_type=jnp.float32)
        + jnp.einsum("jrd,jde->re", received[:, :, cols:], attn_out_parts, preferred_element_type=jnp.float32)
    )
    row_average = jnp.sum(mixed, axis=1, keepdims=True) / width
    square_row = jnp.sum(mixed * mixed, axis=1, keepdims=True) / width
    normed = (
        (mixed - row_average) * lax.rsqrt(square_row - row_average * row_average + 1e-05)
    ).astype(jnp.bfloat16)
    ffn_hidden = jax.nn.relu(
        jnp.dot(normed, ffn_in_full, preferred_element_type=jnp.float32)
    ).astype(jnp.bfloat16)
    out_rows = (
        mixed + jnp.dot(ffn_hidden, ffn_out_full, preferred_element_type=jnp.float32)
    ).astype(jnp.bfloat16)
    out_parts = out_rows.reshape(share, n_mp, cols).transpose(1, 0, 2)
    return lax.all_to_all(out_parts, "mp", 0, 0, tiled=False).reshape(rows, cols)


def solution(mesh):
    return jax.shard_map(
        per_device,
        mesh=mesh,
        in_specs=(
            P("blk", "mp"),
            P("blk"),
            P("blk"),
            P("blk", None, None),
            P(None, "mp"),
            P("mp", None),
            P(None, "mp"),
            P(None, "mp"),
            P(None, "mp"),
            P("mp", None),
            P(None, "mp"),
            P("mp", None),
        ),
        out_specs=P("blk", "mp"),
        check_vma=False,
    )
```

```python
import functools
import math

import jax
import jax.numpy as jnp
from jax import lax
from jax.experimental import pallas as pl
from jax.experimental.pallas import tpu as pltpu
from jax.sharding import PartitionSpec as P

HEAD_DIM = 64
BLOCK = 128
Q_TILE = 512
K_TILE = 4096


def neighbour_sum(features, edge_dst, edge_src, edge_mask, all_features):
    rows, cols = features.shape
    local_blocks = rows // BLOCK
    count = all_features.shape[0] // BLOCK
    blocks = all_features.reshape(count, BLOCK, cols)
    pulled = jnp.take(blocks, jnp.clip(edge_src, 0, count - 1), axis=0)
    summand_terms = jnp.einsum(
        "ers,esf->erf",
        edge_mask.astype(jnp.bfloat16),
        pulled,
        preferred_element_type=jnp.float32,
    )
    target_nodes = (
        edge_dst[:, None] == jnp.arange(local_blocks, dtype=jnp.int32)[None, :]
    ).astype(jnp.float32)
    running_total = jnp.einsum(
        "cy,cla->yla", target_nodes, summand_terms, precision=lax.Precision.HIGHEST
    )
    return running_total.reshape(rows, cols)


def flash_kernel(dim, q_ref, kv_ref, o_ref, m_ref, l_ref, acc_ref):
    j = pl.program_id(1)

    @pl.when(j == 0)
    def _():
        m_ref[...] = jnp.full(m_ref.shape, -jnp.inf, jnp.float32)
        l_ref[...] = jnp.zeros(l_ref.shape, jnp.float32)
        acc_ref[...] = jnp.zeros(acc_ref.shape, jnp.float32)

    kv = kv_ref[...]
    s = lax.dot_general(
        q_ref[...], kv, (((1,), (1,)), ((), ())), preferred_element_type=jnp.float32
    )
    m_prev = m_ref[...]
    m_new = jnp.maximum(m_prev, jnp.max(s, axis=1, keepdims=True))
    alpha = jnp.exp(m_prev - m_new)
    p = jnp.exp(s - m_new)
    l_ref[...] = alpha * l_ref[...] + jnp.sum(p, axis=1, keepdims=True)
    acc_ref[...] = alpha * acc_ref[...] + jnp.dot(
        p.astype(jnp.bfloat16), kv, preferred_element_type=jnp.float32
    )
    m_ref[...] = m_new

    @pl.when(j == pl.num_programs(1) - 1)
    def _():
        o_ref[...] = (acc_ref[:, dim : 2 * dim] / l_ref[...]).astype(o_ref.dtype)


def flash_attention(q, packed_all, head, heads):
    rows, dim = q.shape
    keys_n = packed_all.shape[0]
    tq = min(Q_TILE, rows)
    tk = min(K_TILE, keys_n)
    grid = (rows // tq, keys_n // tk)
    assert heads == 1
    lanes = 2 * dim
    q_pad = jnp.concatenate([q, jnp.zeros((rows, lanes - dim), q.dtype)], axis=1)
    return pl.pallas_call(
        functools.partial(flash_kernel, dim),
        grid=grid,
        in_specs=[
            pl.BlockSpec((tq, lanes), lambda i, j: (i, 0)),
            pl.BlockSpec((tk, lanes), lambda i, j: (j, 0)),
        ],
        out_specs=pl.BlockSpec((tq, dim), lambda i, j: (i, 0)),
        out_shape=jax.ShapeDtypeStruct((rows, dim), jnp.bfloat16),
        scratch_shapes=[
            pltpu.VMEM((tq, 1), jnp.float32),
            pltpu.VMEM((tq, 1), jnp.float32),
            pltpu.VMEM((tq, lanes), jnp.float32),
        ],
        compiler_params=pltpu.CompilerParams(
            dimension_semantics=("arbitrary", "arbitrary")
        ),
        cost_estimate=pl.CostEstimate(
            flops=4 * rows * keys_n * lanes,
            transcendentals=rows * keys_n,
            bytes_accessed=rows * lanes * 2 + grid[0] * keys_n * lanes * 2 + rows * dim * 2,
        ),
    )(q_pad, packed_all)


def gather_kernel(axis, n, x_ref, out_ref, send_sem, recv_sem, local_sem):
    me = lax.axis_index(axis)
    mesh_id = pl.DeviceIdType.MESH
    barrier = pltpu.get_barrier_semaphore()
    for k in range(1, n):
        pl.semaphore_signal(
            barrier, inc=1, device_id={axis: lax.rem(me + k, n)}, device_id_type=mesh_id
        )
    pl.semaphore_wait(barrier, n - 1)
    local = pltpu.make_async_copy(x_ref, out_ref.at[me], local_sem)
    local.start()
    sends = []
    for k in range(1, n):
        copy = pltpu.make_async_remote_copy(
            src_ref=x_ref,
            dst_ref=out_ref.at[me],
            send_sem=send_sem.at[k],
            recv_sem=recv_sem.at[k],
            device_id={axis: lax.rem(me + k, n)},
            device_id_type=mesh_id,
        )
        copy.start()
        sends.append(copy)
    for k in range(1, n):
        source = lax.rem(me + n - k, n)
        arriving = pltpu.make_async_remote_copy(
            src_ref=x_ref,
            dst_ref=out_ref.at[source],
            send_sem=send_sem.at[k],
            recv_sem=recv_sem.at[k],
            device_id={axis: source},
            device_id_type=mesh_id,
        )
        arriving.wait_recv()
    for copy in sends:
        copy.wait_send()
    local.wait()


def dma_all_gather(x, axis, collective_id):
    n = lax.axis_size(axis)
    return pl.pallas_call(
        functools.partial(gather_kernel, axis, n),
        in_specs=[pl.BlockSpec(memory_space=pl.ANY)],
        out_specs=pl.BlockSpec(memory_space=pl.ANY),
        out_shape=jax.ShapeDtypeStruct((n,) + x.shape, x.dtype),
        scratch_shapes=[
            pltpu.SemaphoreType.DMA((n,)),
            pltpu.SemaphoreType.DMA((n,)),
            pltpu.SemaphoreType.DMA,
        ],
        compiler_params=pltpu.CompilerParams(collective_id=collective_id, has_side_effects=True),
    )(x)


def per_device(
    features,
    edge_dst,
    edge_src,
    edge_mask,
    gin_in,
    gin_out,
    w_query,
    w_key,
    w_value,
    w_attn_out,
    ffn_in,
    ffn_out,
):
    rows, cols = features.shape
    n_mp = lax.axis_size("mp")
    width = cols * n_mp
    share = rows // n_mp
    me = lax.axis_index("mp")
    heads = w_query.shape[1] // HEAD_DIM
    scale = 1.0 / math.sqrt(HEAD_DIM)

    all_features = lax.all_gather(features, "blk", axis=0, tiled=True)
    feature_parts = dma_all_gather(features, "mp", 0)

    def project(w):
        return jnp.einsum(
            "jrc,jcd->rd",
            feature_parts,
            w.reshape(n_mp, cols, w.shape[1]),
            preferred_element_type=jnp.float32,
        ).astype(jnp.bfloat16)

    queries = project(w_query) * jnp.bfloat16(scale)
    keys = project(w_key)
    values = project(w_value)
    kv_packed = jnp.concatenate([keys, values], axis=1)
    kv_packed, all_features = lax.optimization_barrier((kv_packed, all_features))
    kv_all = lax.all_gather(kv_packed, "blk", axis=0, tiled=True)

    gathered = neighbour_sum(features, edge_dst, edge_src, edge_mask, all_features)
    local_share = (features.astype(jnp.float32) + gathered * 0.25).astype(jnp.bfloat16)

    pieces = (gin_in.T, ffn_in.T, gin_out, w_attn_out, ffn_out)
    packed_weights = jnp.concatenate(pieces, axis=0)
    kv_all, packed_weights = lax.optimization_barrier((kv_all, packed_weights))
    weight_parts = lax.all_gather(packed_weights, "mp", axis=0, tiled=False)
    unpacked = []
    offset = 0
    for x in pieces:
        unpacked.append(weight_parts[:, offset : offset + x.shape[0], :])
        offset += x.shape[0]
    gin_in_t, ffn_in_t, gin_out_parts, attn_out_parts, ffn_out_parts = unpacked

    attended = flash_attention(queries, kv_all, 0, heads)

    mixed_in = jnp.concatenate([local_share, attended], axis=1).reshape(n_mp, share, -1)
    received = lax.all_to_all(mixed_in, "mp", 0, 0, tiled=False)
    own_rows = (
        lax.dynamic_slice_in_dim(feature_parts, me * share, share, 1)
        .transpose(1, 0, 2)
        .reshape(share, width)
        .astype(jnp.float32)
    )

    local_hidden = jax.nn.relu(
        jnp.einsum(
            "jrc,pqjc->rpq",
            received[:, :, :cols],
            gin_in_t.reshape(n_mp, cols, n_mp, cols),
            preferred_element_type=jnp.float32,
        )
    ).astype(jnp.bfloat16)
    mixed = (
        own_rows
        + jnp.einsum("rjc,jce->re", local_hidden, gin_out_parts, preferred_element_type=jnp.float32)
        + jnp.einsum("jrd,jde->re", received[:, :, cols:], attn_out_parts, preferred_element_type=jnp.float32)
    )
    row_average = jnp.sum(mixed, axis=1, keepdims=True) / width
    square_row = jnp.sum(mixed * mixed, axis=1, keepdims=True) / width
    normed = (
        (mixed - row_average) * lax.rsqrt(square_row - row_average * row_average + 1e-05)
    ).astype(jnp.bfloat16)
    ffn_hidden = jax.nn.relu(
        jnp.einsum("rk,jck->rjc", normed, ffn_in_t, preferred_element_type=jnp.float32)
    ).astype(jnp.bfloat16)
    out_rows = (
        mixed
        + jnp.einsum("rjc,jce->re", ffn_hidden, ffn_out_parts, preferred_element_type=jnp.float32)
    ).astype(jnp.bfloat16)
    out_parts = out_rows.reshape(share, n_mp, cols).transpose(1, 0, 2)
    return lax.all_to_all(out_parts, "mp", 0, 0, tiled=False).reshape(rows, cols)


def solution(mesh):
    return jax.shard_map(
        per_device,
        mesh=mesh,
        in_specs=(
            P("blk", "mp"),
            P("blk"),
            P("blk"),
            P("blk", None, None),
            P(None, "mp"),
            P("mp", None),
            P(None, "mp"),
            P(None, "mp"),
            P(None, "mp"),
            P("mp", None),
            P(None, "mp"),
            P("mp", None),
        ),
        out_specs=P("blk", "mp"),
        check_vma=False,
    )
```

```python
import functools
import math

import jax
import jax.numpy as jnp
from jax import lax
from jax.experimental import pallas as pl
from jax.experimental.pallas import tpu as pltpu
from jax.sharding import PartitionSpec as P

HEAD_DIM = 64
BLOCK = 128
Q_TILE = 512
K_TILE = 4096


def neighbour_sum(features, edge_dst, edge_src, edge_mask, all_features):
    rows, cols = features.shape
    local_blocks = rows // BLOCK
    count = all_features.shape[0] // BLOCK
    blocks = all_features.reshape(count, BLOCK, cols)
    pulled = jnp.take(blocks, jnp.clip(edge_src, 0, count - 1), axis=0)
    summand_terms = jnp.einsum(
        "ers,esf->erf",
        edge_mask.astype(jnp.bfloat16),
        pulled,
        preferred_element_type=jnp.float32,
    )
    target_nodes = (
        edge_dst[:, None] == jnp.arange(local_blocks, dtype=jnp.int32)[None, :]
    ).astype(jnp.float32)
    running_total = jnp.einsum(
        "cy,cla->yla", target_nodes, summand_terms, precision=lax.Precision.HIGHEST
    )
    return running_total.reshape(rows, cols)


def flash_kernel(dim, q_ref, kv_ref, o_ref, m_ref, l_ref, acc_ref):
    j = pl.program_id(1)

    @pl.when(j == 0)
    def _():
        m_ref[...] = jnp.full(m_ref.shape, -jnp.inf, jnp.float32)
        l_ref[...] = jnp.zeros(l_ref.shape, jnp.float32)
        acc_ref[...] = jnp.zeros(acc_ref.shape, jnp.float32)

    kv = kv_ref[...]
    s = lax.dot_general(
        q_ref[...], kv, (((1,), (1,)), ((), ())), preferred_element_type=jnp.float32
    )
    m_prev = m_ref[...]
    m_new = jnp.maximum(m_prev, jnp.max(s, axis=1, keepdims=True))
    alpha = jnp.exp(m_prev - m_new)
    p = jnp.exp(s - m_new)
    l_ref[...] = alpha * l_ref[...] + jnp.sum(p, axis=1, keepdims=True)
    acc_ref[...] = alpha * acc_ref[...] + jnp.dot(
        p.astype(jnp.bfloat16), kv, preferred_element_type=jnp.float32
    )
    m_ref[...] = m_new

    @pl.when(j == pl.num_programs(1) - 1)
    def _():
        o_ref[...] = (acc_ref[:, dim : 2 * dim] / l_ref[...]).astype(o_ref.dtype)


def flash_attention(q, packed_all, head, heads):
    rows, dim = q.shape
    keys_n = packed_all.shape[0]
    tq = min(Q_TILE, rows)
    tk = min(K_TILE, keys_n)
    grid = (rows // tq, keys_n // tk)
    assert heads == 1
    lanes = 2 * dim
    q_pad = jnp.concatenate([q, jnp.zeros((rows, lanes - dim), q.dtype)], axis=1)
    return pl.pallas_call(
        functools.partial(flash_kernel, dim),
        grid=grid,
        in_specs=[
            pl.BlockSpec((tq, lanes), lambda i, j: (i, 0)),
            pl.BlockSpec((tk, lanes), lambda i, j: (j, 0)),
        ],
        out_specs=pl.BlockSpec((tq, dim), lambda i, j: (i, 0)),
        out_shape=jax.ShapeDtypeStruct((rows, dim), jnp.bfloat16),
        scratch_shapes=[
            pltpu.VMEM((tq, 1), jnp.float32),
            pltpu.VMEM((tq, 1), jnp.float32),
            pltpu.VMEM((tq, lanes), jnp.float32),
        ],
        compiler_params=pltpu.CompilerParams(
            dimension_semantics=("arbitrary", "arbitrary")
        ),
        cost_estimate=pl.CostEstimate(
            flops=4 * rows * keys_n * lanes,
            transcendentals=rows * keys_n,
            bytes_accessed=rows * lanes * 2 + grid[0] * keys_n * lanes * 2 + rows * dim * 2,
        ),
    )(q_pad, packed_all)


def gather_kernel(axis, n, x_ref, out_ref, send_sem, recv_sem, local_sem):
    me = lax.axis_index(axis)
    mesh_id = pl.DeviceIdType.MESH
    barrier = pltpu.get_barrier_semaphore()
    for k in range(1, n):
        pl.semaphore_signal(
            barrier, inc=1, device_id={axis: lax.rem(me + k, n)}, device_id_type=mesh_id
        )
    pl.semaphore_wait(barrier, n - 1)
    local = pltpu.make_async_copy(x_ref, out_ref.at[me], local_sem)
    local.start()
    sends = []
    for k in range(1, n):
        copy = pltpu.make_async_remote_copy(
            src_ref=x_ref,
            dst_ref=out_ref.at[me],
            send_sem=send_sem.at[k],
            recv_sem=recv_sem.at[k],
            device_id={axis: lax.rem(me + k, n)},
            device_id_type=mesh_id,
        )
        copy.start()
        sends.append(copy)
    for k in range(1, n):
        source = lax.rem(me + n - k, n)
        arriving = pltpu.make_async_remote_copy(
            src_ref=x_ref,
            dst_ref=out_ref.at[source],
            send_sem=send_sem.at[k],
            recv_sem=recv_sem.at[k],
            device_id={axis: source},
            device_id_type=mesh_id,
        )
        arriving.wait_recv()
    for copy in sends:
        copy.wait_send()
    local.wait()


def dma_all_gather(x, axis, collective_id):
    n = lax.axis_size(axis)
    return pl.pallas_call(
        functools.partial(gather_kernel, axis, n),
        in_specs=[pl.BlockSpec(memory_space=pl.ANY)],
        out_specs=pl.BlockSpec(memory_space=pl.ANY),
        out_shape=jax.ShapeDtypeStruct((n,) + x.shape, x.dtype),
        scratch_shapes=[
            pltpu.SemaphoreType.DMA((n,)),
            pltpu.SemaphoreType.DMA((n,)),
            pltpu.SemaphoreType.DMA,
        ],
        compiler_params=pltpu.CompilerParams(collective_id=collective_id, has_side_effects=True),
    )(x)


def per_device(
    features,
    edge_dst,
    edge_src,
    edge_mask,
    gin_in,
    gin_out,
    w_query,
    w_key,
    w_value,
    w_attn_out,
    ffn_in,
    ffn_out,
):
    rows, cols = features.shape
    n_mp = lax.axis_size("mp")
    width = cols * n_mp
    share = rows // n_mp
    me = lax.axis_index("mp")
    heads = w_query.shape[1] // HEAD_DIM
    scale = 1.0 / math.sqrt(HEAD_DIM)

    feature_parts = dma_all_gather(features, "mp", 0)

    def project(w):
        return jnp.einsum(
            "jrc,jcd->rd",
            feature_parts,
            w.reshape(n_mp, cols, w.shape[1]),
            preferred_element_type=jnp.float32,
        ).astype(jnp.bfloat16)

    queries = project(w_query) * jnp.bfloat16(scale)
    keys = project(w_key)
    values = project(w_value)
    kv_all = lax.all_gather(jnp.concatenate([keys, values], axis=1), "blk", axis=0, tiled=True)

    pieces = (gin_in.T, ffn_in.T, gin_out, w_attn_out, ffn_out)
    packed_weights = jnp.concatenate(pieces, axis=0)
    kv_all, packed_weights, late_features = lax.optimization_barrier((kv_all, packed_weights, features))
    all_features = lax.all_gather(late_features, "blk", axis=0, tiled=True)
    weight_parts = lax.all_gather(packed_weights, "mp", axis=0, tiled=False)
    unpacked = []
    offset = 0
    for x in pieces:
        unpacked.append(weight_parts[:, offset : offset + x.shape[0], :])
        offset += x.shape[0]
    gin_in_t, ffn_in_t, gin_out_parts, attn_out_parts, ffn_out_parts = unpacked

    attended = flash_attention(queries, kv_all, 0, heads)

    gathered = neighbour_sum(features, edge_dst, edge_src, edge_mask, all_features)
    local_share = (features.astype(jnp.float32) + gathered * 0.25).astype(jnp.bfloat16)

    mixed_in = jnp.concatenate([local_share, attended], axis=1).reshape(n_mp, share, -1)
    received = lax.all_to_all(mixed_in, "mp", 0, 0, tiled=False)
    own_rows = (
        lax.dynamic_slice_in_dim(feature_parts, me * share, share, 1)
        .transpose(1, 0, 2)
        .reshape(share, width)
        .astype(jnp.float32)
    )

    local_hidden = jax.nn.relu(
        jnp.einsum(
            "jrc,pqjc->rpq",
            received[:, :, :cols],
            gin_in_t.reshape(n_mp, cols, n_mp, cols),
            preferred_element_type=jnp.float32,
        )
    ).astype(jnp.bfloat16)
    mixed = (
        own_rows
        + jnp.einsum("rjc,jce->re", local_hidden, gin_out_parts, preferred_element_type=jnp.float32)
        + jnp.einsum("jrd,jde->re", received[:, :, cols:], attn_out_parts, preferred_element_type=jnp.float32)
    )
    row_average = jnp.sum(mixed, axis=1, keepdims=True) / width
    square_row = jnp.sum(mixed * mixed, axis=1, keepdims=True) / width
    normed = (
        (mixed - row_average) * lax.rsqrt(square_row - row_average * row_average + 1e-05)
    ).astype(jnp.bfloat16)
    ffn_hidden = jax.nn.relu(
        jnp.einsum("rk,jck->rjc", normed, ffn_in_t, preferred_element_type=jnp.float32)
    ).astype(jnp.bfloat16)
    out_rows = (
        mixed
        + jnp.einsum("rjc,jce->re", ffn_hidden, ffn_out_parts, preferred_element_type=jnp.float32)
    ).astype(jnp.bfloat16)
    out_parts = out_rows.reshape(share, n_mp, cols).transpose(1, 0, 2)
    return lax.all_to_all(out_parts, "mp", 0, 0, tiled=False).reshape(rows, cols)


def solution(mesh):
    return jax.shard_map(
        per_device,
        mesh=mesh,
        in_specs=(
            P("blk", "mp"),
            P("blk"),
            P("blk"),
            P("blk", None, None),
            P(None, "mp"),
            P("mp", None),
            P(None, "mp"),
            P(None, "mp"),
            P(None, "mp"),
            P("mp", None),
            P(None, "mp"),
            P("mp", None),
        ),
        out_specs=P("blk", "mp"),
        check_vma=False,
    )
```

```python
import functools
import math

import jax
import jax.numpy as jnp
from jax import lax
from jax.experimental import pallas as pl
from jax.experimental.pallas import tpu as pltpu
from jax.sharding import PartitionSpec as P

HEAD_DIM = 64
BLOCK = 128
Q_TILE = 512
K_TILE = 4096


def neighbour_sum(features, edge_dst, edge_src, edge_mask, all_features):
    rows, cols = features.shape
    local_blocks = rows // BLOCK
    count = all_features.shape[0] // BLOCK
    blocks = all_features.reshape(count, BLOCK, cols)
    pulled = jnp.take(blocks, jnp.clip(edge_src, 0, count - 1), axis=0)
    summand_terms = jnp.einsum(
        "ers,esf->erf",
        edge_mask.astype(jnp.bfloat16),
        pulled,
        preferred_element_type=jnp.float32,
    )
    target_nodes = (
        edge_dst[:, None] == jnp.arange(local_blocks, dtype=jnp.int32)[None, :]
    ).astype(jnp.float32)
    running_total = jnp.einsum(
        "cy,cla->yla", target_nodes, summand_terms, precision=lax.Precision.HIGHEST
    )
    return running_total.reshape(rows, cols)


def flash_kernel(dim, q_ref, kv_ref, o_ref, m_ref, l_ref, acc_ref):
    j = pl.program_id(1)

    @pl.when(j == 0)
    def _():
        m_ref[...] = jnp.full(m_ref.shape, -jnp.inf, jnp.float32)
        l_ref[...] = jnp.zeros(l_ref.shape, jnp.float32)
        acc_ref[...] = jnp.zeros(acc_ref.shape, jnp.float32)

    kv = kv_ref[...]
    s = lax.dot_general(
        q_ref[...], kv, (((1,), (1,)), ((), ())), preferred_element_type=jnp.float32
    )
    m_prev = m_ref[:, :1]
    m_new = jnp.maximum(m_prev, jnp.max(s, axis=1, keepdims=True))
    alpha = jnp.exp(m_prev - m_new)
    p = jnp.exp(s - m_new)
    l_ref[...] = jnp.broadcast_to(alpha * l_ref[:, :1] + jnp.sum(p, axis=1, keepdims=True), l_ref.shape)
    acc_ref[...] = alpha * acc_ref[...] + jnp.dot(
        p.astype(jnp.bfloat16), kv, preferred_element_type=jnp.float32
    )
    m_ref[...] = jnp.broadcast_to(m_new, m_ref.shape)

    @pl.when(j == pl.num_programs(1) - 1)
    def _():
        o_ref[...] = (acc_ref[:, dim : 2 * dim] / l_ref[:, :1]).astype(o_ref.dtype)


def flash_attention(q, packed_all, head, heads):
    rows, dim = q.shape
    keys_n = packed_all.shape[0]
    tq = min(Q_TILE, rows)
    tk = min(K_TILE, keys_n)
    grid = (rows // tq, keys_n // tk)
    assert heads == 1
    lanes = 2 * dim
    q_pad = jnp.concatenate([q, jnp.zeros((rows, lanes - dim), q.dtype)], axis=1)
    return pl.pallas_call(
        functools.partial(flash_kernel, dim),
        grid=grid,
        in_specs=[
            pl.BlockSpec((tq, lanes), lambda i, j: (i, 0)),
            pl.BlockSpec((tk, lanes), lambda i, j: (j, 0)),
        ],
        out_specs=pl.BlockSpec((tq, dim), lambda i, j: (i, 0)),
        out_shape=jax.ShapeDtypeStruct((rows, dim), jnp.bfloat16),
        scratch_shapes=[
            pltpu.VMEM((tq, 128), jnp.float32),
            pltpu.VMEM((tq, 128), jnp.float32),
            pltpu.VMEM((tq, lanes), jnp.float32),
        ],
        compiler_params=pltpu.CompilerParams(
            dimension_semantics=("arbitrary", "arbitrary")
        ),
        cost_estimate=pl.CostEstimate(
            flops=4 * rows * keys_n * lanes,
            transcendentals=rows * keys_n,
            bytes_accessed=rows * lanes * 2 + grid[0] * keys_n * lanes * 2 + rows * dim * 2,
        ),
    )(q_pad, packed_all)


def exchange_kernel(axis, n, scatter, x_ref, out_ref, send_sem, recv_sem, local_sem):
    me = lax.axis_index(axis)
    mesh_id = pl.DeviceIdType.MESH
    barrier = pltpu.get_barrier_semaphore()
    for k in range(1, n):
        pl.semaphore_signal(
            barrier, inc=1, device_id={axis: lax.rem(me + k, n)}, device_id_type=mesh_id
        )
    pl.semaphore_wait(barrier, n - 1)
    def part(device):
        return x_ref.at[device] if scatter else x_ref

    local = pltpu.make_async_copy(part(me), out_ref.at[me], local_sem)
    local.start()
    sends = []
    for k in range(1, n):
        copy = pltpu.make_async_remote_copy(
            src_ref=part(lax.rem(me + k, n)),
            dst_ref=out_ref.at[me],
            send_sem=send_sem.at[k],
            recv_sem=recv_sem.at[k],
            device_id={axis: lax.rem(me + k, n)},
            device_id_type=mesh_id,
        )
        copy.start()
        sends.append(copy)
    for k in range(1, n):
        source = lax.rem(me + n - k, n)
        arriving = pltpu.make_async_remote_copy(
            src_ref=part(me),
            dst_ref=out_ref.at[source],
            send_sem=send_sem.at[k],
            recv_sem=recv_sem.at[k],
            device_id={axis: source},
            device_id_type=mesh_id,
        )
        arriving.wait_recv()
    for copy in sends:
        copy.wait_send()
    local.wait()


def dma_exchange(x, axis, collective_id, scatter):
    n = lax.axis_size(axis)
    out_shape = x.shape if scatter else (n,) + x.shape
    return pl.pallas_call(
        functools.partial(exchange_kernel, axis, n, scatter),
        in_specs=[pl.BlockSpec(memory_space=pl.ANY)],
        out_specs=pl.BlockSpec(memory_space=pl.ANY),
        out_shape=jax.ShapeDtypeStruct(out_shape, x.dtype),
        scratch_shapes=[
            pltpu.SemaphoreType.DMA((n,)),
            pltpu.SemaphoreType.DMA((n,)),
            pltpu.SemaphoreType.DMA,
        ],
        compiler_params=pltpu.CompilerParams(collective_id=collective_id, has_side_effects=True),
    )(x)


def per_device(
    features,
    edge_dst,
    edge_src,
    edge_mask,
    gin_in,
    gin_out,
    w_query,
    w_key,
    w_value,
    w_attn_out,
    ffn_in,
    ffn_out,
):
    rows, cols = features.shape
    n_mp = lax.axis_size("mp")
    width = cols * n_mp
    share = rows // n_mp
    me = lax.axis_index("mp")
    heads = w_query.shape[1] // HEAD_DIM
    scale = 1.0 / math.sqrt(HEAD_DIM)

    feature_parts = dma_exchange(features, "mp", 0, False)

    def project(w):
        return jnp.einsum(
            "jrc,jcd->rd",
            feature_parts,
            w.reshape(n_mp, cols, w.shape[1]),
            preferred_element_type=jnp.float32,
        ).astype(jnp.bfloat16)

    queries = project(w_query) * jnp.bfloat16(scale)
    keys = project(w_key)
    values = project(w_value)
    kv_all = lax.all_gather(jnp.concatenate([keys, values], axis=1), "blk", axis=0, tiled=True)

    pieces = (gin_in.T, ffn_in.T, gin_out, w_attn_out, ffn_out)
    packed_weights = jnp.concatenate(pieces, axis=0)
    kv_all, packed_weights, late_features = lax.optimization_barrier((kv_all, packed_weights, features))
    all_features = lax.all_gather(late_features, "blk", axis=0, tiled=True)
    weight_parts = lax.all_gather(packed_weights, "mp", axis=0, tiled=False)
    unpacked = []
    offset = 0
    for x in pieces:
        unpacked.append(weight_parts[:, offset : offset + x.shape[0], :])
        offset += x.shape[0]
    gin_in_t, ffn_in_t, gin_out_parts, attn_out_parts, ffn_out_parts = unpacked

    attended = flash_attention(queries, kv_all, 0, heads)

    gathered = neighbour_sum(features, edge_dst, edge_src, edge_mask, all_features)
    local_share = (features.astype(jnp.float32) + gathered * 0.25).astype(jnp.bfloat16)

    mixed_in = jnp.concatenate([local_share, attended], axis=1).reshape(n_mp, share, -1)
    received = dma_exchange(mixed_in, "mp", 1, True)
    own_rows = (
        lax.dynamic_slice_in_dim(feature_parts, me * share, share, 1)
        .transpose(1, 0, 2)
        .reshape(share, width)
        .astype(jnp.float32)
    )

    local_hidden = jax.nn.relu(
        jnp.einsum(
            "jrc,pqjc->rpq",
            received[:, :, :cols],
            gin_in_t.reshape(n_mp, cols, n_mp, cols),
            preferred_element_type=jnp.float32,
        )
    ).astype(jnp.bfloat16)
    mixed = (
        own_rows
        + jnp.einsum("rjc,jce->re", local_hidden, gin_out_parts, preferred_element_type=jnp.float32)
        + jnp.einsum("jrd,jde->re", received[:, :, cols:], attn_out_parts, preferred_element_type=jnp.float32)
    )
    row_average = jnp.sum(mixed, axis=1, keepdims=True) / width
    square_row = jnp.sum(mixed * mixed, axis=1, keepdims=True) / width
    normed = (
        (mixed - row_average) * lax.rsqrt(square_row - row_average * row_average + 1e-05)
    ).astype(jnp.bfloat16)
    ffn_hidden = jax.nn.relu(
        jnp.einsum("rk,jck->rjc", normed, ffn_in_t, preferred_element_type=jnp.float32)
    ).astype(jnp.bfloat16)
    out_rows = (
        mixed
        + jnp.einsum("rjc,jce->re", ffn_hidden, ffn_out_parts, preferred_element_type=jnp.float32)
    ).astype(jnp.bfloat16)
    out_parts = out_rows.reshape(share, n_mp, cols).transpose(1, 0, 2)
    return dma_exchange(out_parts, "mp", 2, True).reshape(rows, cols)


def solution(mesh):
    return jax.shard_map(
        per_device,
        mesh=mesh,
        in_specs=(
            P("blk", "mp"),
            P("blk"),
            P("blk"),
            P("blk", None, None),
            P(None, "mp"),
            P("mp", None),
            P(None, "mp"),
            P(None, "mp"),
            P(None, "mp"),
            P("mp", None),
            P(None, "mp"),
            P("mp", None),
        ),
        out_specs=P("blk", "mp"),
        check_vma=False,
    )
```

```python
import functools
import math

import jax
import jax.numpy as jnp
from jax import lax
from jax.experimental import pallas as pl
from jax.experimental.pallas import tpu as pltpu
from jax.sharding import PartitionSpec as P

HEAD_DIM = 64
BLOCK = 128
Q_TILE = 512
K_TILE = 4096


def neighbour_sum(features, edge_dst, edge_src, edge_mask, all_features):
    rows, cols = features.shape
    local_blocks = rows // BLOCK
    count = all_features.shape[0] // BLOCK
    blocks = all_features.reshape(count, BLOCK, cols)
    pulled = jnp.take(blocks, jnp.clip(edge_src, 0, count - 1), axis=0)
    summand_terms = jnp.einsum(
        "ers,esf->erf",
        edge_mask.astype(jnp.bfloat16),
        pulled,
        preferred_element_type=jnp.float32,
    )
    target_nodes = (
        edge_dst[:, None] == jnp.arange(local_blocks, dtype=jnp.int32)[None, :]
    ).astype(jnp.float32)
    running_total = jnp.einsum(
        "cy,cla->yla", target_nodes, summand_terms, precision=lax.Precision.HIGHEST
    )
    return running_total.reshape(rows, cols)


def flash_kernel(dim, q_ref, kv_ref, o_ref, m_ref, l_ref, acc_ref):
    j = pl.program_id(1)

    @pl.when(j == 0)
    def _():
        m_ref[...] = jnp.full(m_ref.shape, -jnp.inf, jnp.float32)
        l_ref[...] = jnp.zeros(l_ref.shape, jnp.float32)
        acc_ref[...] = jnp.zeros(acc_ref.shape, jnp.float32)

    kv = kv_ref[...]
    s = lax.dot_general(
        q_ref[...], kv, (((1,), (1,)), ((), ())), preferred_element_type=jnp.float32
    )
    m_prev = m_ref[:, :1]
    m_new = jnp.maximum(m_prev, jnp.max(s, axis=1, keepdims=True))
    alpha = jnp.exp(m_prev - m_new)
    p = jnp.exp(s - m_new)
    l_ref[...] = jnp.broadcast_to(alpha * l_ref[:, :1] + jnp.sum(p, axis=1, keepdims=True), l_ref.shape)
    acc_ref[...] = alpha * acc_ref[...] + jnp.dot(
        p.astype(jnp.bfloat16), kv, preferred_element_type=jnp.float32
    )
    m_ref[...] = jnp.broadcast_to(m_new, m_ref.shape)

    @pl.when(j == pl.num_programs(1) - 1)
    def _():
        o_ref[...] = (acc_ref[:, dim : 2 * dim] / l_ref[:, :1]).astype(o_ref.dtype)


def flash_attention(q, packed_all, head, heads):
    rows, dim = q.shape
    keys_n = packed_all.shape[0]
    tq = min(Q_TILE, rows)
    tk = min(K_TILE, keys_n)
    grid = (rows // tq, keys_n // tk)
    assert heads == 1
    lanes = 2 * dim
    q_pad = jnp.concatenate([q, jnp.zeros((rows, lanes - dim), q.dtype)], axis=1)
    return pl.pallas_call(
        functools.partial(flash_kernel, dim),
        grid=grid,
        in_specs=[
            pl.BlockSpec((tq, lanes), lambda i, j: (i, 0)),
            pl.BlockSpec((tk, lanes), lambda i, j: (j, 0)),
        ],
        out_specs=pl.BlockSpec((tq, dim), lambda i, j: (i, 0)),
        out_shape=jax.ShapeDtypeStruct((rows, dim), jnp.bfloat16),
        scratch_shapes=[
            pltpu.VMEM((tq, 128), jnp.float32),
            pltpu.VMEM((tq, 128), jnp.float32),
            pltpu.VMEM((tq, lanes), jnp.float32),
        ],
        compiler_params=pltpu.CompilerParams(
            dimension_semantics=("arbitrary", "arbitrary")
        ),
        cost_estimate=pl.CostEstimate(
            flops=4 * rows * keys_n * lanes,
            transcendentals=rows * keys_n,
            bytes_accessed=rows * lanes * 2 + grid[0] * keys_n * lanes * 2 + rows * dim * 2,
        ),
    )(q_pad, packed_all)


def exchange_kernel(axis, n, scatter, x_ref, out_ref, send_sem, recv_sem, local_sem):
    me = lax.axis_index(axis)
    mesh_id = pl.DeviceIdType.MESH
    barrier = pltpu.get_barrier_semaphore()
    for k in range(1, n):
        pl.semaphore_signal(
            barrier, inc=1, device_id={axis: lax.rem(me + k, n)}, device_id_type=mesh_id
        )
    pl.semaphore_wait(barrier, n - 1)
    def part(device):
        return x_ref.at[device] if scatter else x_ref

    local = pltpu.make_async_copy(part(me), out_ref.at[me], local_sem)
    local.start()
    sends = []
    for k in range(1, n):
        copy = pltpu.make_async_remote_copy(
            src_ref=part(lax.rem(me + k, n)),
            dst_ref=out_ref.at[me],
            send_sem=send_sem.at[k],
            recv_sem=recv_sem.at[k],
            device_id={axis: lax.rem(me + k, n)},
            device_id_type=mesh_id,
        )
        copy.start()
        sends.append(copy)
    for k in range(1, n):
        source = lax.rem(me + n - k, n)
        arriving = pltpu.make_async_remote_copy(
            src_ref=part(me),
            dst_ref=out_ref.at[source],
            send_sem=send_sem.at[k],
            recv_sem=recv_sem.at[k],
            device_id={axis: source},
            device_id_type=mesh_id,
        )
        arriving.wait_recv()
    for copy in sends:
        copy.wait_send()
    local.wait()


def dma_exchange(x, axis, collective_id, scatter):
    n = lax.axis_size(axis)
    out_shape = x.shape if scatter else (n,) + x.shape
    return pl.pallas_call(
        functools.partial(exchange_kernel, axis, n, scatter),
        in_specs=[pl.BlockSpec(memory_space=pl.ANY)],
        out_specs=pl.BlockSpec(memory_space=pl.ANY),
        out_shape=jax.ShapeDtypeStruct(out_shape, x.dtype),
        scratch_shapes=[
            pltpu.SemaphoreType.DMA((n,)),
            pltpu.SemaphoreType.DMA((n,)),
            pltpu.SemaphoreType.DMA,
        ],
        compiler_params=pltpu.CompilerParams(collective_id=collective_id, has_side_effects=True),
    )(x)


def per_device(
    features,
    edge_dst,
    edge_src,
    edge_mask,
    gin_in,
    gin_out,
    w_query,
    w_key,
    w_value,
    w_attn_out,
    ffn_in,
    ffn_out,
):
    rows, cols = features.shape
    n_mp = lax.axis_size("mp")
    width = cols * n_mp
    share = rows // n_mp
    me = lax.axis_index("mp")
    heads = w_query.shape[1] // HEAD_DIM
    scale = 1.0 / math.sqrt(HEAD_DIM)

    feature_parts = dma_exchange(features, "mp", 0, False)

    def project(w):
        return jnp.einsum(
            "jrc,jcd->rd",
            feature_parts,
            w.reshape(n_mp, cols, w.shape[1]),
            preferred_element_type=jnp.float32,
        ).astype(jnp.bfloat16)

    queries = project(w_query) * jnp.bfloat16(scale)
    keys = project(w_key)
    values = project(w_value)
    kv_all = lax.all_gather(jnp.concatenate([keys, values], axis=1), "blk", axis=0, tiled=True)

    pieces = (gin_in.T, ffn_in.T, gin_out, w_attn_out, ffn_out)
    packed_weights = jnp.concatenate(pieces, axis=0)
    kv_all, packed_weights, late_features = lax.optimization_barrier((kv_all, packed_weights, features))
    all_features = lax.all_gather(late_features, "blk", axis=0, tiled=True)
    weight_parts = lax.all_gather(packed_weights, "mp", axis=0, tiled=False)
    unpacked = []
    offset = 0
    for x in pieces:
        unpacked.append(weight_parts[:, offset : offset + x.shape[0], :])
        offset += x.shape[0]
    gin_in_t, ffn_in_t, gin_out_parts, attn_out_parts, ffn_out_parts = unpacked

    attended = flash_attention(queries, kv_all, 0, heads)

    gathered = neighbour_sum(features, edge_dst, edge_src, edge_mask, all_features)
    local_share = (features.astype(jnp.float32) + gathered * 0.25).astype(jnp.bfloat16)

    mixed_in = jnp.concatenate([local_share, attended], axis=1).reshape(n_mp, share, -1)
    received = lax.all_to_all(mixed_in, "mp", 0, 0, tiled=False)
    own_rows = (
        lax.dynamic_slice_in_dim(feature_parts, me * share, share, 1)
        .transpose(1, 0, 2)
        .reshape(share, width)
        .astype(jnp.float32)
    )

    local_hidden = jax.nn.relu(
        jnp.einsum(
            "jrc,pqjc->rpq",
            received[:, :, :cols],
            gin_in_t.reshape(n_mp, cols, n_mp, cols),
            preferred_element_type=jnp.float32,
        )
    ).astype(jnp.bfloat16)
    mixed = (
        own_rows
        + jnp.einsum("rjc,jce->re", local_hidden, gin_out_parts, preferred_element_type=jnp.float32)
        + jnp.einsum("jrd,jde->re", received[:, :, cols:], attn_out_parts, preferred_element_type=jnp.float32)
    )
    row_average = jnp.sum(mixed, axis=1, keepdims=True) / width
    square_row = jnp.sum(mixed * mixed, axis=1, keepdims=True) / width
    normed = (
        (mixed - row_average) * lax.rsqrt(square_row - row_average * row_average + 1e-05)
    ).astype(jnp.bfloat16)
    ffn_hidden = jax.nn.relu(
        jnp.einsum("rk,jck->rjc", normed, ffn_in_t, preferred_element_type=jnp.float32)
    ).astype(jnp.bfloat16)
    out_rows = (
        mixed
        + jnp.einsum("rjc,jce->re", ffn_hidden, ffn_out_parts, preferred_element_type=jnp.float32)
    ).astype(jnp.bfloat16)
    out_parts = out_rows.reshape(share, n_mp, cols).transpose(1, 0, 2)
    return lax.all_to_all(out_parts, "mp", 0, 0, tiled=False).reshape(rows, cols)


def solution(mesh):
    return jax.shard_map(
        per_device,
        mesh=mesh,
        in_specs=(
            P("blk", "mp"),
            P("blk"),
            P("blk"),
            P("blk", None, None),
            P(None, "mp"),
            P("mp", None),
            P(None, "mp"),
            P(None, "mp"),
            P(None, "mp"),
            P("mp", None),
            P(None, "mp"),
            P("mp", None),
        ),
        out_specs=P("blk", "mp"),
        check_vma=False,
    )
```

```python
import functools
import math

import jax
import jax.numpy as jnp
from jax import lax
from jax.experimental import pallas as pl
from jax.experimental.pallas import tpu as pltpu
from jax.sharding import PartitionSpec as P

HEAD_DIM = 64
BLOCK = 128
Q_TILE = 1024
K_TILE = 4096


def neighbour_sum(features, edge_dst, edge_src, edge_mask, all_features):
    rows, cols = features.shape
    local_blocks = rows // BLOCK
    count = all_features.shape[0] // BLOCK
    blocks = all_features.reshape(count, BLOCK, cols)
    pulled = jnp.take(blocks, jnp.clip(edge_src, 0, count - 1), axis=0)
    summand_terms = jnp.einsum(
        "ers,esf->erf",
        edge_mask.astype(jnp.bfloat16),
        pulled,
        preferred_element_type=jnp.float32,
    )
    target_nodes = (
        edge_dst[:, None] == jnp.arange(local_blocks, dtype=jnp.int32)[None, :]
    ).astype(jnp.float32)
    running_total = jnp.einsum(
        "cy,cla->yla", target_nodes, summand_terms, precision=lax.Precision.HIGHEST
    )
    return running_total.reshape(rows, cols)


def flash_kernel(dim, q_ref, kv_ref, o_ref, m_ref, l_ref, acc_ref):
    j = pl.program_id(1)

    @pl.when(j == 0)
    def _():
        m_ref[...] = jnp.full(m_ref.shape, -jnp.inf, jnp.float32)
        l_ref[...] = jnp.zeros(l_ref.shape, jnp.float32)
        acc_ref[...] = jnp.zeros(acc_ref.shape, jnp.float32)

    kv = kv_ref[...]
    s = lax.dot_general(
        q_ref[...], kv, (((1,), (1,)), ((), ())), preferred_element_type=jnp.float32
    )
    m_prev = m_ref[:, :1]
    m_new = jnp.maximum(m_prev, jnp.max(s, axis=1, keepdims=True))
    alpha = jnp.exp(m_prev - m_new)
    p = jnp.exp(s - m_new)
    l_ref[...] = jnp.broadcast_to(alpha * l_ref[:, :1] + jnp.sum(p, axis=1, keepdims=True), l_ref.shape)
    acc_ref[...] = alpha * acc_ref[...] + jnp.dot(
        p.astype(jnp.bfloat16), kv, preferred_element_type=jnp.float32
    )
    m_ref[...] = jnp.broadcast_to(m_new, m_ref.shape)

    @pl.when(j == pl.num_programs(1) - 1)
    def _():
        o_ref[...] = (acc_ref[:, dim : 2 * dim] / l_ref[:, :1]).astype(o_ref.dtype)


def flash_attention(q, packed_all, head, heads):
    rows, dim = q.shape
    keys_n = packed_all.shape[0]
    tq = min(Q_TILE, rows)
    tk = min(K_TILE, keys_n)
    grid = (rows // tq, keys_n // tk)
    assert heads == 1
    lanes = 2 * dim
    q_pad = jnp.concatenate([q, jnp.zeros((rows, lanes - dim), q.dtype)], axis=1)
    return pl.pallas_call(
        functools.partial(flash_kernel, dim),
        grid=grid,
        in_specs=[
            pl.BlockSpec((tq, lanes), lambda i, j: (i, 0)),
            pl.BlockSpec((tk, lanes), lambda i, j: (j, 0)),
        ],
        out_specs=pl.BlockSpec((tq, dim), lambda i, j: (i, 0)),
        out_shape=jax.ShapeDtypeStruct((rows, dim), jnp.bfloat16),
        scratch_shapes=[
            pltpu.VMEM((tq, 128), jnp.float32),
            pltpu.VMEM((tq, 128), jnp.float32),
            pltpu.VMEM((tq, lanes), jnp.float32),
        ],
        compiler_params=pltpu.CompilerParams(
            dimension_semantics=("arbitrary", "arbitrary")
        ),
        cost_estimate=pl.CostEstimate(
            flops=4 * rows * keys_n * lanes,
            transcendentals=rows * keys_n,
            bytes_accessed=rows * lanes * 2 + grid[0] * keys_n * lanes * 2 + rows * dim * 2,
        ),
    )(q_pad, packed_all)


def exchange_kernel(axis, n, scatter, x_ref, out_ref, send_sem, recv_sem, local_sem):
    me = lax.axis_index(axis)
    mesh_id = pl.DeviceIdType.MESH
    barrier = pltpu.get_barrier_semaphore()
    for k in range(1, n):
        pl.semaphore_signal(
            barrier, inc=1, device_id={axis: lax.rem(me + k, n)}, device_id_type=mesh_id
        )
    pl.semaphore_wait(barrier, n - 1)
    def part(device):
        return x_ref.at[device] if scatter else x_ref

    local = pltpu.make_async_copy(part(me), out_ref.at[me], local_sem)
    local.start()
    sends = []
    for k in range(1, n):
        copy = pltpu.make_async_remote_copy(
            src_ref=part(lax.rem(me + k, n)),
            dst_ref=out_ref.at[me],
            send_sem=send_sem.at[k],
            recv_sem=recv_sem.at[k],
            device_id={axis: lax.rem(me + k, n)},
            device_id_type=mesh_id,
        )
        copy.start()
        sends.append(copy)
    for k in range(1, n):
        source = lax.rem(me + n - k, n)
        arriving = pltpu.make_async_remote_copy(
            src_ref=part(me),
            dst_ref=out_ref.at[source],
            send_sem=send_sem.at[k],
            recv_sem=recv_sem.at[k],
            device_id={axis: source},
            device_id_type=mesh_id,
        )
        arriving.wait_recv()
    for copy in sends:
        copy.wait_send()
    local.wait()


def dma_exchange(x, axis, collective_id, scatter):
    n = lax.axis_size(axis)
    out_shape = x.shape if scatter else (n,) + x.shape
    return pl.pallas_call(
        functools.partial(exchange_kernel, axis, n, scatter),
        in_specs=[pl.BlockSpec(memory_space=pltpu.VMEM)],
        out_specs=pl.BlockSpec(memory_space=pl.ANY),
        out_shape=jax.ShapeDtypeStruct(out_shape, x.dtype),
        scratch_shapes=[
            pltpu.SemaphoreType.DMA((n,)),
            pltpu.SemaphoreType.DMA((n,)),
            pltpu.SemaphoreType.DMA,
        ],
        compiler_params=pltpu.CompilerParams(collective_id=collective_id, has_side_effects=True),
    )(x)


def per_device(
    features,
    edge_dst,
    edge_src,
    edge_mask,
    gin_in,
    gin_out,
    w_query,
    w_key,
    w_value,
    w_attn_out,
    ffn_in,
    ffn_out,
):
    rows, cols = features.shape
    n_mp = lax.axis_size("mp")
    width = cols * n_mp
    share = rows // n_mp
    me = lax.axis_index("mp")
    heads = w_query.shape[1] // HEAD_DIM
    scale = 1.0 / math.sqrt(HEAD_DIM)

    feature_parts = dma_exchange(features, "mp", 0, False)

    def project(w):
        return jnp.einsum(
            "jrc,jcd->rd",
            feature_parts,
            w.reshape(n_mp, cols, w.shape[1]),
            preferred_element_type=jnp.float32,
        ).astype(jnp.bfloat16)

    queries = project(w_query) * jnp.bfloat16(scale)
    keys = project(w_key)
    values = project(w_value)
    kv_all = lax.all_gather(jnp.concatenate([keys, values], axis=1), "blk", axis=0, tiled=True)

    pieces = (gin_in.T, ffn_in.T, gin_out, w_attn_out, ffn_out)
    packed_weights = jnp.concatenate(pieces, axis=0)
    kv_all, packed_weights, late_features = lax.optimization_barrier((kv_all, packed_weights, features))
    all_features = lax.all_gather(late_features, "blk", axis=0, tiled=True)
    weight_parts = lax.all_gather(packed_weights, "mp", axis=0, tiled=False)
    unpacked = []
    offset = 0
    for x in pieces:
        unpacked.append(weight_parts[:, offset : offset + x.shape[0], :])
        offset += x.shape[0]
    gin_in_t, ffn_in_t, gin_out_parts, attn_out_parts, ffn_out_parts = unpacked

    attended = flash_attention(queries, kv_all, 0, heads)

    gathered = neighbour_sum(features, edge_dst, edge_src, edge_mask, all_features)
    local_share = (features.astype(jnp.float32) + gathered * 0.25).astype(jnp.bfloat16)

    mixed_in = jnp.concatenate([local_share, attended], axis=1).reshape(n_mp, share, -1)
    received = lax.all_to_all(mixed_in, "mp", 0, 0, tiled=False)
    own_rows = (
        lax.dynamic_slice_in_dim(feature_parts, me * share, share, 1)
        .transpose(1, 0, 2)
        .reshape(share, width)
        .astype(jnp.float32)
    )

    local_hidden = jax.nn.relu(
        jnp.einsum(
            "jrc,pqjc->rpq",
            received[:, :, :cols],
            gin_in_t.reshape(n_mp, cols, n_mp, cols),
            preferred_element_type=jnp.float32,
        )
    ).astype(jnp.bfloat16)
    mixed = (
        own_rows
        + jnp.einsum("rjc,jce->re", local_hidden, gin_out_parts, preferred_element_type=jnp.float32)
        + jnp.einsum("jrd,jde->re", received[:, :, cols:], attn_out_parts, preferred_element_type=jnp.float32)
    )
    row_average = jnp.sum(mixed, axis=1, keepdims=True) / width
    square_row = jnp.sum(mixed * mixed, axis=1, keepdims=True) / width
    normed = (
        (mixed - row_average) * lax.rsqrt(square_row - row_average * row_average + 1e-05)
    ).astype(jnp.bfloat16)
    ffn_hidden = jax.nn.relu(
        jnp.einsum("rk,jck->rjc", normed, ffn_in_t, preferred_element_type=jnp.float32)
    ).astype(jnp.bfloat16)
    out_rows = (
        mixed
        + jnp.einsum("rjc,jce->re", ffn_hidden, ffn_out_parts, preferred_element_type=jnp.float32)
    ).astype(jnp.bfloat16)
    out_parts = out_rows.reshape(share, n_mp, cols).transpose(1, 0, 2)
    return lax.all_to_all(out_parts, "mp", 0, 0, tiled=False).reshape(rows, cols)


def solution(mesh):
    return jax.shard_map(
        per_device,
        mesh=mesh,
        in_specs=(
            P("blk", "mp"),
            P("blk"),
            P("blk"),
            P("blk", None, None),
            P(None, "mp"),
            P("mp", None),
            P(None, "mp"),
            P(None, "mp"),
            P(None, "mp"),
            P("mp", None),
            P(None, "mp"),
            P("mp", None),
        ),
        out_specs=P("blk", "mp"),
        check_vma=False,
    )
```

```python
import functools
import math

import jax
import jax.numpy as jnp
from jax import lax
from jax.experimental import pallas as pl
from jax.experimental.pallas import tpu as pltpu
from jax.sharding import PartitionSpec as P

HEAD_DIM = 64
BLOCK = 128
Q_TILE = 1024
K_TILE = 4096


def neighbour_sum(features, edge_dst, edge_src, edge_mask, all_features):
    rows, cols = features.shape
    local_blocks = rows // BLOCK
    count = all_features.shape[0] // BLOCK
    blocks = all_features.reshape(count, BLOCK, cols)
    pulled = jnp.take(blocks, jnp.clip(edge_src, 0, count - 1), axis=0)
    summand_terms = jnp.einsum(
        "ers,esf->erf",
        edge_mask.astype(jnp.bfloat16),
        pulled,
        preferred_element_type=jnp.float32,
    )
    target_nodes = (
        edge_dst[:, None] == jnp.arange(local_blocks, dtype=jnp.int32)[None, :]
    ).astype(jnp.float32)
    running_total = jnp.einsum(
        "cy,cla->yla", target_nodes, summand_terms, precision=lax.Precision.HIGHEST
    )
    return running_total.reshape(rows, cols)


def flash_kernel(dim, q_ref, kv_ref, o_ref, m_ref, l_ref, acc_ref):
    j = pl.program_id(1)

    @pl.when(j == 0)
    def _():
        m_ref[...] = jnp.full(m_ref.shape, -jnp.inf, jnp.float32)
        l_ref[...] = jnp.zeros(l_ref.shape, jnp.float32)
        acc_ref[...] = jnp.zeros(acc_ref.shape, jnp.float32)

    kv = kv_ref[...]
    s = lax.dot_general(
        q_ref[...], kv, (((1,), (1,)), ((), ())), preferred_element_type=jnp.float32
    )
    m_prev = m_ref[:, :1]
    m_new = jnp.maximum(m_prev, jnp.max(s, axis=1, keepdims=True))
    alpha = jnp.exp(m_prev - m_new)
    p = jnp.exp(s - m_new)
    l_ref[...] = jnp.broadcast_to(alpha * l_ref[:, :1] + jnp.sum(p, axis=1, keepdims=True), l_ref.shape)
    acc_ref[...] = alpha * acc_ref[...] + jnp.dot(
        p.astype(jnp.bfloat16), kv, preferred_element_type=jnp.float32
    )
    m_ref[...] = jnp.broadcast_to(m_new, m_ref.shape)

    @pl.when(j == pl.num_programs(1) - 1)
    def _():
        o_ref[...] = (acc_ref[:, dim : 2 * dim] / l_ref[:, :1]).astype(o_ref.dtype)


def flash_attention(q, packed_all, head, heads):
    rows, dim = q.shape
    keys_n = packed_all.shape[0]
    tq = min(Q_TILE, rows)
    tk = min(K_TILE, keys_n)
    grid = (rows // tq, keys_n // tk)
    assert heads == 1
    lanes = 2 * dim
    q_pad = jnp.concatenate([q, jnp.zeros((rows, lanes - dim), q.dtype)], axis=1)
    return pl.pallas_call(
        functools.partial(flash_kernel, dim),
        grid=grid,
        in_specs=[
            pl.BlockSpec((tq, lanes), lambda i, j: (i, 0)),
            pl.BlockSpec((tk, lanes), lambda i, j: (j, 0)),
        ],
        out_specs=pl.BlockSpec((tq, dim), lambda i, j: (i, 0)),
        out_shape=jax.ShapeDtypeStruct((rows, dim), jnp.bfloat16),
        scratch_shapes=[
            pltpu.VMEM((tq, 128), jnp.float32),
            pltpu.VMEM((tq, 128), jnp.float32),
            pltpu.VMEM((tq, lanes), jnp.float32),
        ],
        compiler_params=pltpu.CompilerParams(
            dimension_semantics=("arbitrary", "arbitrary")
        ),
        cost_estimate=pl.CostEstimate(
            flops=4 * rows * keys_n * lanes,
            transcendentals=rows * keys_n,
            bytes_accessed=rows * lanes * 2 + grid[0] * keys_n * lanes * 2 + rows * dim * 2,
        ),
    )(q_pad, packed_all)


def exchange_kernel(axis, n, scatter, x_ref, out_ref, send_sem, recv_sem, local_sem):
    me = lax.axis_index(axis)
    mesh_id = pl.DeviceIdType.MESH
    barrier = pltpu.get_barrier_semaphore()
    for k in range(1, n):
        pl.semaphore_signal(
            barrier, inc=1, device_id={axis: lax.rem(me + k, n)}, device_id_type=mesh_id
        )
    pl.semaphore_wait(barrier, n - 1)
    def part(device):
        return x_ref.at[device] if scatter else x_ref

    local = pltpu.make_async_copy(part(me), out_ref.at[me], local_sem)
    local.start()
    sends = []
    for k in range(1, n):
        copy = pltpu.make_async_remote_copy(
            src_ref=part(lax.rem(me + k, n)),
            dst_ref=out_ref.at[me],
            send_sem=send_sem.at[k],
            recv_sem=recv_sem.at[k],
            device_id={axis: lax.rem(me + k, n)},
            device_id_type=mesh_id,
        )
        copy.start()
        sends.append(copy)
    for k in range(1, n):
        source = lax.rem(me + n - k, n)
        arriving = pltpu.make_async_remote_copy(
            src_ref=part(me),
            dst_ref=out_ref.at[source],
            send_sem=send_sem.at[k],
            recv_sem=recv_sem.at[k],
            device_id={axis: source},
            device_id_type=mesh_id,
        )
        arriving.wait_recv()
    for copy in sends:
        copy.wait_send()
    local.wait()


def dma_exchange(x, axis, collective_id, scatter):
    n = lax.axis_size(axis)
    out_shape = x.shape if scatter else (n,) + x.shape
    return pl.pallas_call(
        functools.partial(exchange_kernel, axis, n, scatter),
        in_specs=[pl.BlockSpec(memory_space=pltpu.VMEM)],
        out_specs=pl.BlockSpec(memory_space=pl.ANY),
        out_shape=jax.ShapeDtypeStruct(out_shape, x.dtype),
        scratch_shapes=[
            pltpu.SemaphoreType.DMA((n,)),
            pltpu.SemaphoreType.DMA((n,)),
            pltpu.SemaphoreType.DMA,
        ],
        compiler_params=pltpu.CompilerParams(collective_id=collective_id, has_side_effects=True),
    )(x)


def per_device(
    features,
    edge_dst,
    edge_src,
    edge_mask,
    gin_in,
    gin_out,
    w_query,
    w_key,
    w_value,
    w_attn_out,
    ffn_in,
    ffn_out,
):
    rows, cols = features.shape
    n_mp = lax.axis_size("mp")
    width = cols * n_mp
    share = rows // n_mp
    me = lax.axis_index("mp")
    heads = w_query.shape[1] // HEAD_DIM
    scale = 1.0 / math.sqrt(HEAD_DIM)

    feature_parts = dma_exchange(features, "mp", 0, False)

    def project(w):
        return jnp.einsum(
            "jrc,jcd->rd",
            feature_parts,
            w.reshape(n_mp, cols, w.shape[1]),
            preferred_element_type=jnp.float32,
        ).astype(jnp.bfloat16)

    queries = project(w_query) * jnp.bfloat16(scale)
    keys = project(w_key)
    values = project(w_value)
    kv_all = lax.all_gather(jnp.concatenate([keys, values], axis=1), "blk", axis=0, tiled=True)

    pieces = (gin_in.T, ffn_in.T, gin_out, w_attn_out, ffn_out)
    packed_weights = jnp.concatenate(pieces, axis=0)
    packed_weights, _ = lax.optimization_barrier((packed_weights, feature_parts))
    by_offset = [packed_weights] + [
        lax.ppermute(packed_weights, "mp", [(i, (i + k) % n_mp) for i in range(n_mp)])
        for k in range(1, n_mp)
    ]
    kv_all, late_features = lax.optimization_barrier((kv_all, features))
    all_features = lax.all_gather(late_features, "blk", axis=0, tiled=True)
    attended = flash_attention(queries, kv_all, 0, heads)
    attended, by_offset = lax.optimization_barrier((attended, by_offset))
    source_order = (me - jnp.arange(n_mp, dtype=jnp.int32)) % n_mp
    weight_parts = jnp.take(jnp.stack(by_offset), source_order, axis=0)
    unpacked = []
    offset = 0
    for x in pieces:
        unpacked.append(weight_parts[:, offset : offset + x.shape[0], :])
        offset += x.shape[0]
    gin_in_t, ffn_in_t, gin_out_parts, attn_out_parts, ffn_out_parts = unpacked

    gathered = neighbour_sum(features, edge_dst, edge_src, edge_mask, all_features)
    local_share = (features.astype(jnp.float32) + gathered * 0.25).astype(jnp.bfloat16)

    mixed_in = jnp.concatenate([local_share, attended], axis=1).reshape(n_mp, share, -1)
    received = lax.all_to_all(mixed_in, "mp", 0, 0, tiled=False)
    own_rows = (
        lax.dynamic_slice_in_dim(feature_parts, me * share, share, 1)
        .transpose(1, 0, 2)
        .reshape(share, width)
        .astype(jnp.float32)
    )

    local_hidden = jax.nn.relu(
        jnp.einsum(
            "jrc,pqjc->rpq",
            received[:, :, :cols],
            gin_in_t.reshape(n_mp, cols, n_mp, cols),
            preferred_element_type=jnp.float32,
        )
    ).astype(jnp.bfloat16)
    mixed = (
        own_rows
        + jnp.einsum("rjc,jce->re", local_hidden, gin_out_parts, preferred_element_type=jnp.float32)
        + jnp.einsum("jrd,jde->re", received[:, :, cols:], attn_out_parts, preferred_element_type=jnp.float32)
    )
    row_average = jnp.sum(mixed, axis=1, keepdims=True) / width
    square_row = jnp.sum(mixed * mixed, axis=1, keepdims=True) / width
    normed = (
        (mixed - row_average) * lax.rsqrt(square_row - row_average * row_average + 1e-05)
    ).astype(jnp.bfloat16)
    ffn_hidden = jax.nn.relu(
        jnp.einsum("rk,jck->rjc", normed, ffn_in_t, preferred_element_type=jnp.float32)
    ).astype(jnp.bfloat16)
    out_rows = (
        mixed
        + jnp.einsum("rjc,jce->re", ffn_hidden, ffn_out_parts, preferred_element_type=jnp.float32)
    ).astype(jnp.bfloat16)
    out_parts = out_rows.reshape(share, n_mp, cols).transpose(1, 0, 2)
    return lax.all_to_all(out_parts, "mp", 0, 0, tiled=False).reshape(rows, cols)


def solution(mesh):
    return jax.shard_map(
        per_device,
        mesh=mesh,
        in_specs=(
            P("blk", "mp"),
            P("blk"),
            P("blk"),
            P("blk", None, None),
            P(None, "mp"),
            P("mp", None),
            P(None, "mp"),
            P(None, "mp"),
            P(None, "mp"),
            P("mp", None),
            P(None, "mp"),
            P("mp", None),
        ),
        out_specs=P("blk", "mp"),
        check_vma=False,
    )
```

```python
import functools
import math

import jax
import jax.numpy as jnp
from jax import lax
from jax.experimental import pallas as pl
from jax.experimental.pallas import tpu as pltpu
from jax.sharding import PartitionSpec as P

HEAD_DIM = 64
BLOCK = 128
Q_TILE = 512
K_TILE = 4096


def neighbour_sum(features, edge_dst, edge_src, edge_mask, all_features):
    rows, cols = features.shape
    local_blocks = rows // BLOCK
    count = all_features.shape[0] // BLOCK
    blocks = all_features.reshape(count, BLOCK, cols)
    pulled = jnp.take(blocks, jnp.clip(edge_src, 0, count - 1), axis=0)
    summand_terms = jnp.einsum(
        "ers,esf->erf",
        edge_mask.astype(jnp.bfloat16),
        pulled,
        preferred_element_type=jnp.float32,
    )
    target_nodes = (
        edge_dst[:, None] == jnp.arange(local_blocks, dtype=jnp.int32)[None, :]
    ).astype(jnp.float32)
    running_total = jnp.einsum(
        "cy,cla->yla", target_nodes, summand_terms, precision=lax.Precision.HIGHEST
    )
    return running_total.reshape(rows, cols)


def flash_kernel(dim, q_ref, kv_ref, o_ref, m_ref, l_ref, acc_ref):
    j = pl.program_id(1)

    @pl.when(j == 0)
    def _():
        m_ref[...] = jnp.full(m_ref.shape, -jnp.inf, jnp.float32)
        l_ref[...] = jnp.zeros(l_ref.shape, jnp.float32)
        acc_ref[...] = jnp.zeros(acc_ref.shape, jnp.float32)

    kv = kv_ref[...]
    s = lax.dot_general(
        q_ref[...], kv, (((1,), (1,)), ((), ())), preferred_element_type=jnp.float32
    )
    m_prev = m_ref[:, :1]
    m_new = jnp.maximum(m_prev, jnp.max(s, axis=1, keepdims=True))
    alpha = jnp.exp(m_prev - m_new)
    p = jnp.exp(s - m_new)
    l_ref[...] = jnp.broadcast_to(alpha * l_ref[:, :1] + jnp.sum(p, axis=1, keepdims=True), l_ref.shape)
    acc_ref[...] = alpha * acc_ref[...] + jnp.dot(
        p.astype(jnp.bfloat16), kv, preferred_element_type=jnp.float32
    )
    m_ref[...] = jnp.broadcast_to(m_new, m_ref.shape)

    @pl.when(j == pl.num_programs(1) - 1)
    def _():
        o_ref[...] = (acc_ref[:, dim : 2 * dim] / l_ref[:, :1]).astype(o_ref.dtype)


def flash_attention(q, packed_all, head, heads):
    rows, dim = q.shape
    keys_n = packed_all.shape[0]
    tq = min(Q_TILE, rows)
    tk = min(K_TILE, keys_n)
    grid = (rows // tq, keys_n // tk)
    assert heads == 1
    lanes = 2 * dim
    q_pad = jnp.concatenate([q, jnp.zeros((rows, lanes - dim), q.dtype)], axis=1)
    return pl.pallas_call(
        functools.partial(flash_kernel, dim),
        grid=grid,
        in_specs=[
            pl.BlockSpec((tq, lanes), lambda i, j: (i, 0)),
            pl.BlockSpec((tk, lanes), lambda i, j: (j, 0)),
        ],
        out_specs=pl.BlockSpec((tq, dim), lambda i, j: (i, 0)),
        out_shape=jax.ShapeDtypeStruct((rows, dim), jnp.bfloat16),
        scratch_shapes=[
            pltpu.VMEM((tq, 128), jnp.float32),
            pltpu.VMEM((tq, 128), jnp.float32),
            pltpu.VMEM((tq, lanes), jnp.float32),
        ],
        compiler_params=pltpu.CompilerParams(
            dimension_semantics=("arbitrary", "arbitrary")
        ),
        cost_estimate=pl.CostEstimate(
            flops=4 * rows * keys_n * lanes,
            transcendentals=rows * keys_n,
            bytes_accessed=rows * lanes * 2 + grid[0] * keys_n * lanes * 2 + rows * dim * 2,
        ),
    )(q_pad, packed_all)


def exchange_kernel(axis, n, scatter, x_ref, out_ref, send_sem, recv_sem, local_sem):
    me = lax.axis_index(axis)
    mesh_id = pl.DeviceIdType.MESH
    barrier = pltpu.get_barrier_semaphore()
    for k in range(1, n):
        pl.semaphore_signal(
            barrier, inc=1, device_id={axis: lax.rem(me + k, n)}, device_id_type=mesh_id
        )
    pl.semaphore_wait(barrier, n - 1)
    def part(device):
        return x_ref.at[device] if scatter else x_ref

    local = pltpu.make_async_copy(part(me), out_ref.at[me], local_sem)
    local.start()
    sends = []
    for k in range(1, n):
        copy = pltpu.make_async_remote_copy(
            src_ref=part(lax.rem(me + k, n)),
            dst_ref=out_ref.at[me],
            send_sem=send_sem.at[k],
            recv_sem=recv_sem.at[k],
            device_id={axis: lax.rem(me + k, n)},
            device_id_type=mesh_id,
        )
        copy.start()
        sends.append(copy)
    for k in range(1, n):
        source = lax.rem(me + n - k, n)
        arriving = pltpu.make_async_remote_copy(
            src_ref=part(me),
            dst_ref=out_ref.at[source],
            send_sem=send_sem.at[k],
            recv_sem=recv_sem.at[k],
            device_id={axis: source},
            device_id_type=mesh_id,
        )
        arriving.wait_recv()
    for copy in sends:
        copy.wait_send()
    local.wait()


def dma_exchange(x, axis, collective_id, scatter):
    n = lax.axis_size(axis)
    out_shape = x.shape if scatter else (n,) + x.shape
    return pl.pallas_call(
        functools.partial(exchange_kernel, axis, n, scatter),
        in_specs=[pl.BlockSpec(memory_space=pl.ANY)],
        out_specs=pl.BlockSpec(memory_space=pl.ANY),
        out_shape=jax.ShapeDtypeStruct(out_shape, x.dtype),
        scratch_shapes=[
            pltpu.SemaphoreType.DMA((n,)),
            pltpu.SemaphoreType.DMA((n,)),
            pltpu.SemaphoreType.DMA,
        ],
        compiler_params=pltpu.CompilerParams(collective_id=collective_id, has_side_effects=True),
    )(x)


def per_device(
    features,
    edge_dst,
    edge_src,
    edge_mask,
    gin_in,
    gin_out,
    w_query,
    w_key,
    w_value,
    w_attn_out,
    ffn_in,
    ffn_out,
):
    rows, cols = features.shape
    n_mp = lax.axis_size("mp")
    width = cols * n_mp
    share = rows // n_mp
    me = lax.axis_index("mp")
    heads = w_query.shape[1] // HEAD_DIM
    scale = 1.0 / math.sqrt(HEAD_DIM)

    feature_parts = dma_exchange(features, "mp", 0, False)

    def project(w):
        return jnp.einsum(
            "jrc,jcd->rd",
            feature_parts,
            w.reshape(n_mp, cols, w.shape[1]),
            preferred_element_type=jnp.float32,
        ).astype(jnp.bfloat16)

    projected = project(jnp.concatenate([w_query, w_key, w_value], axis=1))
    queries = projected[:, : HEAD_DIM * heads] * jnp.bfloat16(scale)
    kv_all = lax.all_gather(projected[:, HEAD_DIM * heads :], "blk", axis=0, tiled=True)

    pieces = (gin_in.T, ffn_in.T, gin_out, w_attn_out, ffn_out)
    packed_weights = jnp.concatenate(pieces, axis=0)
    kv_all, packed_weights, late_features = lax.optimization_barrier((kv_all, packed_weights, features))
    all_features = lax.all_gather(late_features, "blk", axis=0, tiled=True)
    weight_parts = lax.all_gather(packed_weights, "mp", axis=0, tiled=False)
    unpacked = []
    offset = 0
    for x in pieces:
        unpacked.append(weight_parts[:, offset : offset + x.shape[0], :])
        offset += x.shape[0]
    gin_in_t, ffn_in_t, gin_out_parts, attn_out_parts, ffn_out_parts = unpacked

    attended = flash_attention(queries, kv_all, 0, heads)

    gathered = neighbour_sum(features, edge_dst, edge_src, edge_mask, all_features)
    local_share = (features.astype(jnp.float32) + gathered * 0.25).astype(jnp.bfloat16)

    mixed_in = jnp.concatenate([local_share, attended], axis=1).reshape(n_mp, share, -1)
    received = lax.all_to_all(mixed_in, "mp", 0, 0, tiled=False)
    own_rows = (
        lax.dynamic_slice_in_dim(feature_parts, me * share, share, 1)
        .transpose(1, 0, 2)
        .reshape(share, width)
        .astype(jnp.float32)
    )

    local_hidden = jax.nn.relu(
        jnp.einsum(
            "jrc,pqjc->rpq",
            received[:, :, :cols],
            gin_in_t.reshape(n_mp, cols, n_mp, cols),
            preferred_element_type=jnp.float32,
        )
    ).astype(jnp.bfloat16)
    mixed = (
        own_rows
        + jnp.einsum("rjc,jce->re", local_hidden, gin_out_parts, preferred_element_type=jnp.float32)
        + jnp.einsum("jrd,jde->re", received[:, :, cols:], attn_out_parts, preferred_element_type=jnp.float32)
    )
    row_average = jnp.sum(mixed, axis=1, keepdims=True) / width
    square_row = jnp.sum(mixed * mixed, axis=1, keepdims=True) / width
    normed = (
        (mixed - row_average) * lax.rsqrt(square_row - row_average * row_average + 1e-05)
    ).astype(jnp.bfloat16)
    ffn_hidden = jax.nn.relu(
        jnp.einsum("rk,jck->rjc", normed, ffn_in_t, preferred_element_type=jnp.float32)
    ).astype(jnp.bfloat16)
    out_rows = (
        mixed
        + jnp.einsum("rjc,jce->re", ffn_hidden, ffn_out_parts, preferred_element_type=jnp.float32)
    ).astype(jnp.bfloat16)
    out_parts = out_rows.reshape(share, n_mp, cols).transpose(1, 0, 2)
    return lax.all_to_all(out_parts, "mp", 0, 0, tiled=False).reshape(rows, cols)


def solution(mesh):
    return jax.shard_map(
        per_device,
        mesh=mesh,
        in_specs=(
            P("blk", "mp"),
            P("blk"),
            P("blk"),
            P("blk", None, None),
            P(None, "mp"),
            P("mp", None),
            P(None, "mp"),
            P(None, "mp"),
            P(None, "mp"),
            P("mp", None),
            P(None, "mp"),
            P("mp", None),
        ),
        out_specs=P("blk", "mp"),
        check_vma=False,
    )
```

```python
import functools
import math

import jax
import jax.numpy as jnp
from jax import lax
from jax.experimental import pallas as pl
from jax.experimental.pallas import tpu as pltpu
from jax.sharding import PartitionSpec as P

HEAD_DIM = 64
BLOCK = 128
Q_TILE = 512
K_TILE = 4096


def neighbour_sum(features, edge_dst, edge_src, edge_mask, all_features):
    rows, cols = features.shape
    local_blocks = rows // BLOCK
    count = all_features.shape[0] // BLOCK
    blocks = all_features.reshape(count, BLOCK, cols)
    pulled = jnp.take(blocks, jnp.clip(edge_src, 0, count - 1), axis=0)
    summand_terms = jnp.einsum(
        "ers,esf->erf",
        edge_mask.astype(jnp.bfloat16),
        pulled,
        preferred_element_type=jnp.float32,
    )
    target_nodes = (
        edge_dst[:, None] == jnp.arange(local_blocks, dtype=jnp.int32)[None, :]
    ).astype(jnp.float32)
    running_total = jnp.einsum(
        "cy,cla->yla", target_nodes, summand_terms, precision=lax.Precision.HIGHEST
    )
    return running_total.reshape(rows, cols)


def flash_kernel(dim, q_ref, kv_ref, o_ref, m_ref, l_ref, acc_ref):
    j = pl.program_id(1)

    @pl.when(j == 0)
    def _():
        m_ref[...] = jnp.full(m_ref.shape, -jnp.inf, jnp.float32)
        l_ref[...] = jnp.zeros(l_ref.shape, jnp.float32)
        acc_ref[...] = jnp.zeros(acc_ref.shape, jnp.float32)

    kv = kv_ref[...]
    s = lax.dot_general(
        q_ref[...], kv, (((1,), (1,)), ((), ())), preferred_element_type=jnp.float32
    )
    m_prev = m_ref[:, :1]
    m_new = jnp.maximum(m_prev, jnp.max(s, axis=1, keepdims=True))
    alpha = jnp.exp(m_prev - m_new)
    p = jnp.exp(s - m_new)
    l_ref[...] = jnp.broadcast_to(alpha * l_ref[:, :1] + jnp.sum(p, axis=1, keepdims=True), l_ref.shape)
    acc_ref[...] = alpha * acc_ref[...] + jnp.dot(
        p.astype(jnp.bfloat16), kv, preferred_element_type=jnp.float32
    )
    m_ref[...] = jnp.broadcast_to(m_new, m_ref.shape)

    @pl.when(j == pl.num_programs(1) - 1)
    def _():
        o_ref[...] = (acc_ref[:, dim : 2 * dim] / l_ref[:, :1]).astype(o_ref.dtype)


def flash_attention(q, packed_all, head, heads):
    rows, dim = q.shape
    keys_n = packed_all.shape[0]
    tq = min(Q_TILE, rows)
    tk = min(K_TILE, keys_n)
    grid = (rows // tq, keys_n // tk)
    assert heads == 1
    lanes = 2 * dim
    q_pad = jnp.concatenate([q, jnp.zeros((rows, lanes - dim), q.dtype)], axis=1)
    return pl.pallas_call(
        functools.partial(flash_kernel, dim),
        grid=grid,
        in_specs=[
            pl.BlockSpec((tq, lanes), lambda i, j: (i, 0)),
            pl.BlockSpec((tk, lanes), lambda i, j: (j, 0)),
        ],
        out_specs=pl.BlockSpec((tq, dim), lambda i, j: (i, 0)),
        out_shape=jax.ShapeDtypeStruct((rows, dim), jnp.bfloat16),
        scratch_shapes=[
            pltpu.VMEM((tq, 128), jnp.float32),
            pltpu.VMEM((tq, 128), jnp.float32),
            pltpu.VMEM((tq, lanes), jnp.float32),
        ],
        compiler_params=pltpu.CompilerParams(
            dimension_semantics=("arbitrary", "arbitrary")
        ),
        cost_estimate=pl.CostEstimate(
            flops=4 * rows * keys_n * lanes,
            transcendentals=rows * keys_n,
            bytes_accessed=rows * lanes * 2 + grid[0] * keys_n * lanes * 2 + rows * dim * 2,
        ),
    )(q_pad, packed_all)


def exchange_kernel(axis, n, scatter, x_ref, out_ref, send_sem, recv_sem, local_sem):
    me = lax.axis_index(axis)
    mesh_id = pl.DeviceIdType.MESH
    barrier = pltpu.get_barrier_semaphore()
    for k in range(1, n):
        pl.semaphore_signal(
            barrier, inc=1, device_id={axis: lax.rem(me + k, n)}, device_id_type=mesh_id
        )
    pl.semaphore_wait(barrier, n - 1)
    def part(device):
        return x_ref.at[device] if scatter else x_ref

    local = pltpu.make_async_copy(part(me), out_ref.at[me], local_sem)
    local.start()
    sends = []
    for k in range(1, n):
        copy = pltpu.make_async_remote_copy(
            src_ref=part(lax.rem(me + k, n)),
            dst_ref=out_ref.at[me],
            send_sem=send_sem.at[k],
            recv_sem=recv_sem.at[k],
            device_id={axis: lax.rem(me + k, n)},
            device_id_type=mesh_id,
        )
        copy.start()
        sends.append(copy)
    for k in range(1, n):
        source = lax.rem(me + n - k, n)
        arriving = pltpu.make_async_remote_copy(
            src_ref=part(me),
            dst_ref=out_ref.at[source],
            send_sem=send_sem.at[k],
            recv_sem=recv_sem.at[k],
            device_id={axis: source},
            device_id_type=mesh_id,
        )
        arriving.wait_recv()
    for copy in sends:
        copy.wait_send()
    local.wait()


def dma_exchange(x, axis, collective_id, scatter):
    n = lax.axis_size(axis)
    out_shape = x.shape if scatter else (n,) + x.shape
    return pl.pallas_call(
        functools.partial(exchange_kernel, axis, n, scatter),
        in_specs=[pl.BlockSpec(memory_space=pl.ANY)],
        out_specs=pl.BlockSpec(memory_space=pl.ANY),
        out_shape=jax.ShapeDtypeStruct(out_shape, x.dtype),
        scratch_shapes=[
            pltpu.SemaphoreType.DMA((n,)),
            pltpu.SemaphoreType.DMA((n,)),
            pltpu.SemaphoreType.DMA,
        ],
        compiler_params=pltpu.CompilerParams(collective_id=collective_id, has_side_effects=True),
    )(x)


def per_device(
    features,
    edge_dst,
    edge_src,
    edge_mask,
    gin_in,
    gin_out,
    w_query,
    w_key,
    w_value,
    w_attn_out,
    ffn_in,
    ffn_out,
):
    rows, cols = features.shape
    n_mp = lax.axis_size("mp")
    width = cols * n_mp
    share = rows // n_mp
    me = lax.axis_index("mp")
    heads = w_query.shape[1] // HEAD_DIM
    scale = 1.0 / math.sqrt(HEAD_DIM)

    feature_parts = dma_exchange(features, "mp", 0, False)

    def project(w):
        return jnp.einsum(
            "jrc,jcd->rd",
            feature_parts,
            w.reshape(n_mp, cols, w.shape[1]),
            preferred_element_type=jnp.float32,
        ).astype(jnp.bfloat16)

    projected = project(jnp.concatenate([w_query, w_key, w_value], axis=1))
    queries = projected[:, : HEAD_DIM * heads] * jnp.bfloat16(scale)
    kv_all = lax.all_gather(projected[:, HEAD_DIM * heads :], "blk", axis=0, tiled=True)

    pieces = (gin_in.T, ffn_in.T, gin_out, w_attn_out, ffn_out)
    packed_weights = jnp.concatenate(pieces, axis=0)
    n_blk = lax.axis_size("blk")
    piece_rows = packed_weights.shape[0] // n_blk
    piece = lax.dynamic_slice_in_dim(
        packed_weights, lax.axis_index("blk") * piece_rows, piece_rows, 0
    )
    piece_parts = lax.all_gather(piece, "mp", axis=0, tiled=False)
    kv_all, piece_parts, late_features = lax.optimization_barrier((kv_all, piece_parts, features))
    all_features = lax.all_gather(late_features, "blk", axis=0, tiled=True)
    weight_parts = lax.all_gather(piece_parts, "blk", axis=1, tiled=True)
    unpacked = []
    offset = 0
    for x in pieces:
        unpacked.append(weight_parts[:, offset : offset + x.shape[0], :])
        offset += x.shape[0]
    gin_in_t, ffn_in_t, gin_out_parts, attn_out_parts, ffn_out_parts = unpacked

    attended = flash_attention(queries, kv_all, 0, heads)

    gathered = neighbour_sum(features, edge_dst, edge_src, edge_mask, all_features)
    local_share = (features.astype(jnp.float32) + gathered * 0.25).astype(jnp.bfloat16)

    mixed_in = jnp.concatenate([local_share, attended], axis=1).reshape(n_mp, share, -1)
    received = lax.all_to_all(mixed_in, "mp", 0, 0, tiled=False)
    own_rows = (
        lax.dynamic_slice_in_dim(feature_parts, me * share, share, 1)
        .transpose(1, 0, 2)
        .reshape(share, width)
        .astype(jnp.float32)
    )

    local_hidden = jax.nn.relu(
        jnp.einsum(
            "jrc,pqjc->rpq",
            received[:, :, :cols],
            gin_in_t.reshape(n_mp, cols, n_mp, cols),
            preferred_element_type=jnp.float32,
        )
    ).astype(jnp.bfloat16)
    mixed = (
        own_rows
        + jnp.einsum("rjc,jce->re", local_hidden, gin_out_parts, preferred_element_type=jnp.float32)
        + jnp.einsum("jrd,jde->re", received[:, :, cols:], attn_out_parts, preferred_element_type=jnp.float32)
    )
    row_average = jnp.sum(mixed, axis=1, keepdims=True) / width
    square_row = jnp.sum(mixed * mixed, axis=1, keepdims=True) / width
    normed = (
        (mixed - row_average) * lax.rsqrt(square_row - row_average * row_average + 1e-05)
    ).astype(jnp.bfloat16)
    ffn_hidden = jax.nn.relu(
        jnp.einsum("rk,jck->rjc", normed, ffn_in_t, preferred_element_type=jnp.float32)
    ).astype(jnp.bfloat16)
    out_rows = (
        mixed
        + jnp.einsum("rjc,jce->re", ffn_hidden, ffn_out_parts, preferred_element_type=jnp.float32)
    ).astype(jnp.bfloat16)
    out_parts = out_rows.reshape(share, n_mp, cols).transpose(1, 0, 2)
    return lax.all_to_all(out_parts, "mp", 0, 0, tiled=False).reshape(rows, cols)


def solution(mesh):
    return jax.shard_map(
        per_device,
        mesh=mesh,
        in_specs=(
            P("blk", "mp"),
            P("blk"),
            P("blk"),
            P("blk", None, None),
            P(None, "mp"),
            P("mp", None),
            P(None, "mp"),
            P(None, "mp"),
            P(None, "mp"),
            P("mp", None),
            P(None, "mp"),
            P("mp", None),
        ),
        out_specs=P("blk", "mp"),
        check_vma=False,
    )
```

```python
import functools
import math

import jax
import jax.numpy as jnp
from jax import lax
from jax.experimental import pallas as pl
from jax.experimental.pallas import tpu as pltpu
from jax.sharding import PartitionSpec as P

HEAD_DIM = 64
BLOCK = 128
Q_TILE = 1024
K_TILE = 4096


def neighbour_sum(features, edge_dst, edge_src, edge_mask, all_features):
    rows, cols = features.shape
    local_blocks = rows // BLOCK
    count = all_features.shape[0]
    blocks = all_features
    pulled = jnp.take(blocks, jnp.clip(edge_src, 0, count - 1), axis=0)
    summand_terms = jnp.einsum(
        "ers,esf->erf",
        edge_mask.astype(jnp.bfloat16),
        pulled,
        preferred_element_type=jnp.float32,
    )
    target_nodes = (
        edge_dst[:, None] == jnp.arange(local_blocks, dtype=jnp.int32)[None, :]
    ).astype(jnp.float32)
    running_total = jnp.einsum(
        "cy,cla->yla", target_nodes, summand_terms, precision=lax.Precision.HIGHEST
    )
    return running_total.reshape(rows, cols)


def flash_kernel(dim, q_ref, kv_ref, o_ref, m_ref, l_ref, acc_ref):
    j = pl.program_id(1)

    @pl.when(j == 0)
    def _():
        m_ref[...] = jnp.full(m_ref.shape, -jnp.inf, jnp.float32)
        l_ref[...] = jnp.zeros(l_ref.shape, jnp.float32)
        acc_ref[...] = jnp.zeros(acc_ref.shape, jnp.float32)

    kv = kv_ref[...]
    s = lax.dot_general(
        q_ref[...], kv, (((1,), (1,)), ((), ())), preferred_element_type=jnp.float32
    )
    m_prev = m_ref[:, :1]
    m_new = jnp.maximum(m_prev, jnp.max(s, axis=1, keepdims=True))
    alpha = jnp.exp(m_prev - m_new)
    p = jnp.exp(s - m_new)
    l_ref[...] = jnp.broadcast_to(alpha * l_ref[:, :1] + jnp.sum(p, axis=1, keepdims=True), l_ref.shape)
    acc_ref[...] = alpha * acc_ref[...] + jnp.dot(
        p.astype(jnp.bfloat16), kv, preferred_element_type=jnp.float32
    )
    m_ref[...] = jnp.broadcast_to(m_new, m_ref.shape)

    @pl.when(j == pl.num_programs(1) - 1)
    def _():
        o_ref[...] = (acc_ref[:, dim : 2 * dim] / l_ref[:, :1]).astype(o_ref.dtype)


def flash_attention(q, packed_all, head, heads):
    rows, dim = q.shape
    keys_n = packed_all.shape[0]
    tq = min(Q_TILE, rows)
    tk = min(K_TILE, keys_n)
    grid = (rows // tq, keys_n // tk)
    assert heads == 1
    lanes = 2 * dim
    q_pad = jnp.concatenate([q, jnp.zeros((rows, lanes - dim), q.dtype)], axis=1)
    return pl.pallas_call(
        functools.partial(flash_kernel, dim),
        grid=grid,
        in_specs=[
            pl.BlockSpec((tq, lanes), lambda i, j: (i, 0)),
            pl.BlockSpec((tk, lanes), lambda i, j: (j, 0)),
        ],
        out_specs=pl.BlockSpec((tq, dim), lambda i, j: (i, 0)),
        out_shape=jax.ShapeDtypeStruct((rows, dim), jnp.bfloat16),
        scratch_shapes=[
            pltpu.VMEM((tq, 128), jnp.float32),
            pltpu.VMEM((tq, 128), jnp.float32),
            pltpu.VMEM((tq, lanes), jnp.float32),
        ],
        compiler_params=pltpu.CompilerParams(
            dimension_semantics=("arbitrary", "arbitrary")
        ),
        cost_estimate=pl.CostEstimate(
            flops=4 * rows * keys_n * lanes,
            transcendentals=rows * keys_n,
            bytes_accessed=rows * lanes * 2 + grid[0] * keys_n * lanes * 2 + rows * dim * 2,
        ),
    )(q_pad, packed_all)


def exchange_kernel(axis, n, scatter, x_ref, out_ref, send_sem, recv_sem, local_sem):
    me = lax.axis_index(axis)
    mesh_id = pl.DeviceIdType.MESH
    barrier = pltpu.get_barrier_semaphore()
    for k in range(1, n):
        pl.semaphore_signal(
            barrier, inc=1, device_id={axis: lax.rem(me + k, n)}, device_id_type=mesh_id
        )
    pl.semaphore_wait(barrier, n - 1)
    def part(device):
        return x_ref.at[device] if scatter else x_ref

    local = pltpu.make_async_copy(part(me), out_ref.at[me], local_sem)
    local.start()
    sends = []
    for k in range(1, n):
        copy = pltpu.make_async_remote_copy(
            src_ref=part(lax.rem(me + k, n)),
            dst_ref=out_ref.at[me],
            send_sem=send_sem.at[k],
            recv_sem=recv_sem.at[k],
            device_id={axis: lax.rem(me + k, n)},
            device_id_type=mesh_id,
        )
        copy.start()
        sends.append(copy)
    for k in range(1, n):
        source = lax.rem(me + n - k, n)
        arriving = pltpu.make_async_remote_copy(
            src_ref=part(me),
            dst_ref=out_ref.at[source],
            send_sem=send_sem.at[k],
            recv_sem=recv_sem.at[k],
            device_id={axis: source},
            device_id_type=mesh_id,
        )
        arriving.wait_recv()
    for copy in sends:
        copy.wait_send()
    local.wait()


def dma_exchange(x, axis, collective_id, scatter):
    n = lax.axis_size(axis)
    out_shape = x.shape if scatter else (n,) + x.shape
    return pl.pallas_call(
        functools.partial(exchange_kernel, axis, n, scatter),
        in_specs=[pl.BlockSpec(memory_space=pl.ANY)],
        out_specs=pl.BlockSpec(memory_space=pl.ANY),
        out_shape=jax.ShapeDtypeStruct(out_shape, x.dtype),
        scratch_shapes=[
            pltpu.SemaphoreType.DMA((n,)),
            pltpu.SemaphoreType.DMA((n,)),
            pltpu.SemaphoreType.DMA,
        ],
        compiler_params=pltpu.CompilerParams(collective_id=collective_id, has_side_effects=True),
    )(x)


def per_device(
    features,
    edge_dst,
    edge_src,
    edge_mask,
    gin_in,
    gin_out,
    w_query,
    w_key,
    w_value,
    w_attn_out,
    ffn_in,
    ffn_out,
):
    rows, cols = features.shape
    n_mp = lax.axis_size("mp")
    width = cols * n_mp
    share = rows // n_mp
    me = lax.axis_index("mp")
    heads = w_query.shape[1] // HEAD_DIM
    scale = 1.0 / math.sqrt(HEAD_DIM)

    feature_parts = dma_exchange(features, "mp", 0, False)

    def project(w):
        return jnp.einsum(
            "jrc,jcd->rd",
            feature_parts,
            w.reshape(n_mp, cols, w.shape[1]),
            preferred_element_type=jnp.float32,
        ).astype(jnp.bfloat16)

    projected = project(jnp.concatenate([w_query, w_key, w_value], axis=1))
    queries = projected[:, : HEAD_DIM * heads] * jnp.bfloat16(scale)
    kv_all = lax.all_gather(projected[:, HEAD_DIM * heads :], "blk", axis=0, tiled=True)

    pieces = (gin_in.T, ffn_in.T, gin_out, w_attn_out, ffn_out)
    packed_weights = jnp.concatenate(pieces, axis=0)
    n_blk = lax.axis_size("blk")
    piece_rows = packed_weights.shape[0] // n_blk
    piece = lax.dynamic_slice_in_dim(
        packed_weights, lax.axis_index("blk") * piece_rows, piece_rows, 0
    )
    piece_parts = lax.all_gather(piece, "mp", axis=0, tiled=False)
    kv_all, piece_parts, late_features = lax.optimization_barrier((kv_all, piece_parts, features))
    all_features = lax.all_gather(
        late_features.reshape(rows // BLOCK, BLOCK, cols), "blk", axis=0, tiled=True
    )
    weight_parts = lax.all_gather(piece_parts, "blk", axis=1, tiled=True)
    unpacked = []
    offset = 0
    for x in pieces:
        unpacked.append(weight_parts[:, offset : offset + x.shape[0], :])
        offset += x.shape[0]
    gin_in_t, ffn_in_t, gin_out_parts, attn_out_parts, ffn_out_parts = unpacked

    attended = flash_attention(queries, kv_all, 0, heads)

    gathered = neighbour_sum(features, edge_dst, edge_src, edge_mask, all_features)
    local_share = (features.astype(jnp.float32) + gathered * 0.25).astype(jnp.bfloat16)

    mixed_in = jnp.concatenate([local_share, attended], axis=1).reshape(n_mp, share, -1)
    received = lax.all_to_all(mixed_in, "mp", 0, 0, tiled=False)
    own_rows = (
        lax.dynamic_slice_in_dim(feature_parts, me * share, share, 1)
        .transpose(1, 0, 2)
        .reshape(share, width)
        .astype(jnp.float32)
    )

    local_hidden = jax.nn.relu(
        jnp.einsum(
            "jrc,pqjc->rpq",
            received[:, :, :cols],
            gin_in_t.reshape(n_mp, cols, n_mp, cols),
            preferred_element_type=jnp.float32,
        )
    ).astype(jnp.bfloat16)
    mixed = (
        own_rows
        + jnp.einsum("rjc,jce->re", local_hidden, gin_out_parts, preferred_element_type=jnp.float32)
        + jnp.einsum("jrd,jde->re", received[:, :, cols:], attn_out_parts, preferred_element_type=jnp.float32)
    )
    row_average = jnp.sum(mixed, axis=1, keepdims=True) / width
    square_row = jnp.sum(mixed * mixed, axis=1, keepdims=True) / width
    normed = (
        (mixed - row_average) * lax.rsqrt(square_row - row_average * row_average + 1e-05)
    ).astype(jnp.bfloat16)
    ffn_hidden = jax.nn.relu(
        jnp.einsum("rk,jck->rjc", normed, ffn_in_t, preferred_element_type=jnp.float32)
    ).astype(jnp.bfloat16)
    out_rows = (
        mixed
        + jnp.einsum("rjc,jce->re", ffn_hidden, ffn_out_parts, preferred_element_type=jnp.float32)
    ).astype(jnp.bfloat16)
    out_parts = out_rows.reshape(share, n_mp, cols).transpose(1, 0, 2)
    return lax.all_to_all(out_parts, "mp", 0, 0, tiled=False).reshape(rows, cols)


def solution(mesh):
    return jax.shard_map(
        per_device,
        mesh=mesh,
        in_specs=(
            P("blk", "mp"),
            P("blk"),
            P("blk"),
            P("blk", None, None),
            P(None, "mp"),
            P("mp", None),
            P(None, "mp"),
            P(None, "mp"),
            P(None, "mp"),
            P("mp", None),
            P(None, "mp"),
            P("mp", None),
        ),
        out_specs=P("blk", "mp"),
        check_vma=False,
    )
```

```python
import functools
import math

import jax
import jax.numpy as jnp
from jax import lax
from jax.experimental import pallas as pl
from jax.experimental.pallas import tpu as pltpu
from jax.sharding import PartitionSpec as P

HEAD_DIM = 64
BLOCK = 128
Q_TILE = 1024
K_TILE = 4096


def neighbour_sum(features, edge_dst, edge_src, edge_mask, all_features):
    rows, cols = features.shape
    local_blocks = rows // BLOCK
    count = all_features.shape[0]
    blocks = all_features
    pulled = jnp.take(blocks, jnp.clip(edge_src, 0, count - 1), axis=0)
    summand_terms = jnp.einsum(
        "ers,esf->erf",
        edge_mask.astype(jnp.bfloat16),
        pulled,
        preferred_element_type=jnp.float32,
    )
    target_nodes = (
        edge_dst[:, None] == jnp.arange(local_blocks, dtype=jnp.int32)[None, :]
    ).astype(jnp.float32)
    running_total = jnp.einsum(
        "cy,cla->yla", target_nodes, summand_terms, precision=lax.Precision.HIGHEST
    )
    return running_total.reshape(rows, cols)


def flash_kernel(dim, q_ref, kv_ref, o_ref, m_ref, l_ref, acc_ref):
    j = pl.program_id(1)

    @pl.when(j == 0)
    def _():
        m_ref[...] = jnp.full(m_ref.shape, -jnp.inf, jnp.float32)
        l_ref[...] = jnp.zeros(l_ref.shape, jnp.float32)
        acc_ref[...] = jnp.zeros(acc_ref.shape, jnp.float32)

    kv = kv_ref[...]
    s = lax.dot_general(
        q_ref[...], kv, (((1,), (1,)), ((), ())), preferred_element_type=jnp.float32
    )
    m_prev = m_ref[:, :1]
    m_new = jnp.maximum(m_prev, jnp.max(s, axis=1, keepdims=True))
    alpha = jnp.exp(m_prev - m_new)
    p = jnp.exp(s - m_new)
    l_ref[...] = jnp.broadcast_to(alpha * l_ref[:, :1] + jnp.sum(p, axis=1, keepdims=True), l_ref.shape)
    acc_ref[...] = alpha * acc_ref[...] + jnp.dot(
        p.astype(jnp.bfloat16), kv, preferred_element_type=jnp.float32
    )
    m_ref[...] = jnp.broadcast_to(m_new, m_ref.shape)

    @pl.when(j == pl.num_programs(1) - 1)
    def _():
        o_ref[...] = (acc_ref[:, dim : 2 * dim] / l_ref[:, :1]).astype(o_ref.dtype)


def flash_attention(q, packed_all, head, heads):
    rows, dim = q.shape
    keys_n = packed_all.shape[0]
    tq = min(Q_TILE, rows)
    tk = min(K_TILE, keys_n)
    grid = (rows // tq, keys_n // tk)
    assert heads == 1
    lanes = 2 * dim
    q_pad = jnp.concatenate([q, jnp.zeros((rows, lanes - dim), q.dtype)], axis=1)
    return pl.pallas_call(
        functools.partial(flash_kernel, dim),
        grid=grid,
        in_specs=[
            pl.BlockSpec((tq, lanes), lambda i, j: (i, 0)),
            pl.BlockSpec((tk, lanes), lambda i, j: (j, 0)),
        ],
        out_specs=pl.BlockSpec((tq, dim), lambda i, j: (i, 0)),
        out_shape=jax.ShapeDtypeStruct((rows, dim), jnp.bfloat16),
        scratch_shapes=[
            pltpu.VMEM((tq, 128), jnp.float32),
            pltpu.VMEM((tq, 128), jnp.float32),
            pltpu.VMEM((tq, lanes), jnp.float32),
        ],
        compiler_params=pltpu.CompilerParams(
            dimension_semantics=("arbitrary", "arbitrary")
        ),
        cost_estimate=pl.CostEstimate(
            flops=4 * rows * keys_n * lanes,
            transcendentals=rows * keys_n,
            bytes_accessed=rows * lanes * 2 + grid[0] * keys_n * lanes * 2 + rows * dim * 2,
        ),
    )(q_pad, packed_all)


def exchange_kernel(axis, n, scatter, x_ref, out_ref, send_sem, recv_sem, local_sem):
    me = lax.axis_index(axis)
    mesh_id = pl.DeviceIdType.MESH
    barrier = pltpu.get_barrier_semaphore()
    for k in range(1, n):
        pl.semaphore_signal(
            barrier, inc=1, device_id={axis: lax.rem(me + k, n)}, device_id_type=mesh_id
        )
    pl.semaphore_wait(barrier, n - 1)
    def part(device):
        return x_ref.at[device] if scatter else x_ref

    local = pltpu.make_async_copy(part(me), out_ref.at[me], local_sem)
    local.start()
    sends = []
    for k in range(1, n):
        copy = pltpu.make_async_remote_copy(
            src_ref=part(lax.rem(me + k, n)),
            dst_ref=out_ref.at[me],
            send_sem=send_sem.at[k],
            recv_sem=recv_sem.at[k],
            device_id={axis: lax.rem(me + k, n)},
            device_id_type=mesh_id,
        )
        copy.start()
        sends.append(copy)
    for k in range(1, n):
        source = lax.rem(me + n - k, n)
        arriving = pltpu.make_async_remote_copy(
            src_ref=part(me),
            dst_ref=out_ref.at[source],
            send_sem=send_sem.at[k],
            recv_sem=recv_sem.at[k],
            device_id={axis: source},
            device_id_type=mesh_id,
        )
        arriving.wait_recv()
    for copy in sends:
        copy.wait_send()
    local.wait()


def dma_exchange(x, axis, collective_id, scatter):
    n = lax.axis_size(axis)
    out_shape = x.shape if scatter else (n,) + x.shape
    return pl.pallas_call(
        functools.partial(exchange_kernel, axis, n, scatter),
        in_specs=[pl.BlockSpec(memory_space=pl.ANY)],
        out_specs=pl.BlockSpec(memory_space=pl.ANY),
        out_shape=jax.ShapeDtypeStruct(out_shape, x.dtype),
        scratch_shapes=[
            pltpu.SemaphoreType.DMA((n,)),
            pltpu.SemaphoreType.DMA((n,)),
            pltpu.SemaphoreType.DMA,
        ],
        compiler_params=pltpu.CompilerParams(collective_id=collective_id, has_side_effects=True),
    )(x)


def per_device(
    features,
    edge_dst,
    edge_src,
    edge_mask,
    gin_in,
    gin_out,
    w_query,
    w_key,
    w_value,
    w_attn_out,
    ffn_in,
    ffn_out,
):
    rows, cols = features.shape
    n_mp = lax.axis_size("mp")
    width = cols * n_mp
    share = rows // n_mp
    me = lax.axis_index("mp")
    heads = w_query.shape[1] // HEAD_DIM
    scale = 1.0 / math.sqrt(HEAD_DIM)

    feature_parts = dma_exchange(
        features.reshape(rows * cols // 128, 128), "mp", 0, False
    ).reshape(n_mp, rows, cols)

    def project(w):
        return jnp.einsum(
            "jrc,jcd->rd",
            feature_parts,
            w.reshape(n_mp, cols, w.shape[1]),
            preferred_element_type=jnp.float32,
        ).astype(jnp.bfloat16)

    projected = project(jnp.concatenate([w_query, w_key, w_value], axis=1))
    queries = projected[:, : HEAD_DIM * heads] * jnp.bfloat16(scale)
    kv_all = lax.all_gather(projected[:, HEAD_DIM * heads :], "blk", axis=0, tiled=True)

    pieces = (gin_in.T, ffn_in.T, gin_out, w_attn_out, ffn_out)
    packed_weights = jnp.concatenate(pieces, axis=0)
    n_blk = lax.axis_size("blk")
    piece_rows = packed_weights.shape[0] // n_blk
    piece = lax.dynamic_slice_in_dim(
        packed_weights, lax.axis_index("blk") * piece_rows, piece_rows, 0
    )
    piece_parts = lax.all_gather(piece, "mp", axis=0, tiled=False)
    kv_all, piece_parts, late_features = lax.optimization_barrier((kv_all, piece_parts, features))
    all_features = lax.all_gather(
        late_features.reshape(rows // BLOCK, BLOCK, cols), "blk", axis=0, tiled=True
    )
    weight_parts = lax.all_gather(piece_parts, "blk", axis=1, tiled=True)
    unpacked = []
    offset = 0
    for x in pieces:
        unpacked.append(weight_parts[:, offset : offset + x.shape[0], :])
        offset += x.shape[0]
    gin_in_t, ffn_in_t, gin_out_parts, attn_out_parts, ffn_out_parts = unpacked

    attended = flash_attention(queries, kv_all, 0, heads)

    gathered = neighbour_sum(features, edge_dst, edge_src, edge_mask, all_features)
    local_share = (features.astype(jnp.float32) + gathered * 0.25).astype(jnp.bfloat16)

    mixed_in = jnp.concatenate([local_share, attended], axis=1).reshape(n_mp, share, -1)
    received = lax.all_to_all(mixed_in, "mp", 0, 0, tiled=False)
    own_rows = (
        lax.dynamic_slice_in_dim(feature_parts, me * share, share, 1)
        .transpose(1, 0, 2)
        .reshape(share, width)
        .astype(jnp.float32)
    )

    local_hidden = jax.nn.relu(
        jnp.einsum(
            "jrc,pqjc->rpq",
            received[:, :, :cols],
            gin_in_t.reshape(n_mp, cols, n_mp, cols),
            preferred_element_type=jnp.float32,
        )
    ).astype(jnp.bfloat16)
    mixed = (
        own_rows
        + jnp.einsum("rjc,jce->re", local_hidden, gin_out_parts, preferred_element_type=jnp.float32)
        + jnp.einsum("jrd,jde->re", received[:, :, cols:], attn_out_parts, preferred_element_type=jnp.float32)
    )
    row_average = jnp.sum(mixed, axis=1, keepdims=True) / width
    square_row = jnp.sum(mixed * mixed, axis=1, keepdims=True) / width
    normed = (
        (mixed - row_average) * lax.rsqrt(square_row - row_average * row_average + 1e-05)
    ).astype(jnp.bfloat16)
    ffn_hidden = jax.nn.relu(
        jnp.einsum("rk,jck->rjc", normed, ffn_in_t, preferred_element_type=jnp.float32)
    ).astype(jnp.bfloat16)
    out_rows = (
        mixed
        + jnp.einsum("rjc,jce->re", ffn_hidden, ffn_out_parts, preferred_element_type=jnp.float32)
    ).astype(jnp.bfloat16)
    out_parts = out_rows.reshape(share, n_mp, cols).transpose(1, 0, 2)
    return lax.all_to_all(out_parts, "mp", 0, 0, tiled=False).reshape(rows, cols)


def solution(mesh):
    return jax.shard_map(
        per_device,
        mesh=mesh,
        in_specs=(
            P("blk", "mp"),
            P("blk"),
            P("blk"),
            P("blk", None, None),
            P(None, "mp"),
            P("mp", None),
            P(None, "mp"),
            P(None, "mp"),
            P(None, "mp"),
            P("mp", None),
            P(None, "mp"),
            P("mp", None),
        ),
        out_specs=P("blk", "mp"),
        check_vma=False,
    )
```

```python
import functools
import math

import jax
import jax.numpy as jnp
from jax import lax
from jax.experimental import pallas as pl
from jax.experimental.pallas import tpu as pltpu
from jax.sharding import PartitionSpec as P

HEAD_DIM = 64
BLOCK = 128
Q_TILE = 1024
K_TILE = 4096


def neighbour_sum(features, edge_dst, edge_src, edge_mask, all_features):
    rows, cols = features.shape
    local_blocks = rows // BLOCK
    count = all_features.shape[0]
    blocks = all_features
    pulled = jnp.take(blocks, jnp.clip(edge_src, 0, count - 1), axis=0)
    summand_terms = jnp.einsum(
        "ers,esf->erf",
        edge_mask.astype(jnp.bfloat16),
        pulled,
        preferred_element_type=jnp.float32,
    )
    target_nodes = (
        edge_dst[:, None] == jnp.arange(local_blocks, dtype=jnp.int32)[None, :]
    ).astype(jnp.float32)
    running_total = jnp.einsum(
        "cy,cla->yla", target_nodes, summand_terms, precision=lax.Precision.HIGHEST
    )
    return running_total.reshape(rows, cols)


def flash_kernel(dim, q_ref, kv_ref, o_ref, m_ref, l_ref, acc_ref):
    j = pl.program_id(1)

    @pl.when(j == 0)
    def _():
        m_ref[...] = jnp.full(m_ref.shape, -jnp.inf, jnp.float32)
        l_ref[...] = jnp.zeros(l_ref.shape, jnp.float32)
        acc_ref[...] = jnp.zeros(acc_ref.shape, jnp.float32)

    kv = kv_ref[...]
    s = lax.dot_general(
        q_ref[...], kv, (((1,), (1,)), ((), ())), preferred_element_type=jnp.float32
    )
    m_prev = m_ref[:, :1]
    m_new = jnp.maximum(m_prev, jnp.max(s, axis=1, keepdims=True))
    alpha = jnp.exp(m_prev - m_new)
    p = jnp.exp(s - m_new)
    l_ref[...] = jnp.broadcast_to(alpha * l_ref[:, :1] + jnp.sum(p, axis=1, keepdims=True), l_ref.shape)
    acc_ref[...] = alpha * acc_ref[...] + jnp.dot(
        p.astype(jnp.bfloat16), kv, preferred_element_type=jnp.float32
    )
    m_ref[...] = jnp.broadcast_to(m_new, m_ref.shape)

    @pl.when(j == pl.num_programs(1) - 1)
    def _():
        o_ref[...] = (acc_ref[:, dim : 2 * dim] / l_ref[:, :1]).astype(o_ref.dtype)


def flash_attention(q, packed_all, head, heads):
    rows, dim = q.shape
    keys_n = packed_all.shape[0]
    tq = min(Q_TILE, rows)
    tk = min(K_TILE, keys_n)
    grid = (rows // tq, keys_n // tk)
    assert heads == 1
    lanes = 2 * dim
    q_pad = jnp.concatenate([q, jnp.zeros((rows, lanes - dim), q.dtype)], axis=1)
    return pl.pallas_call(
        functools.partial(flash_kernel, dim),
        grid=grid,
        in_specs=[
            pl.BlockSpec((tq, lanes), lambda i, j: (i, 0)),
            pl.BlockSpec((tk, lanes), lambda i, j: (j, 0)),
        ],
        out_specs=pl.BlockSpec((tq, dim), lambda i, j: (i, 0)),
        out_shape=jax.ShapeDtypeStruct((rows, dim), jnp.bfloat16),
        scratch_shapes=[
            pltpu.VMEM((tq, 128), jnp.float32),
            pltpu.VMEM((tq, 128), jnp.float32),
            pltpu.VMEM((tq, lanes), jnp.float32),
        ],
        compiler_params=pltpu.CompilerParams(
            dimension_semantics=("arbitrary", "arbitrary")
        ),
        cost_estimate=pl.CostEstimate(
            flops=4 * rows * keys_n * lanes,
            transcendentals=rows * keys_n,
            bytes_accessed=rows * lanes * 2 + grid[0] * keys_n * lanes * 2 + rows * dim * 2,
        ),
    )(q_pad, packed_all)


def exchange_kernel(axis, n, scatter, x_ref, out_ref, send_sem, recv_sem, local_sem):
    me = lax.axis_index(axis)
    mesh_id = pl.DeviceIdType.MESH
    barrier = pltpu.get_barrier_semaphore()
    for k in range(1, n):
        pl.semaphore_signal(
            barrier, inc=1, device_id={axis: lax.rem(me + k, n)}, device_id_type=mesh_id
        )
    pl.semaphore_wait(barrier, n - 1)
    def part(device):
        return x_ref.at[device] if scatter else x_ref

    local = pltpu.make_async_copy(part(me), out_ref.at[me], local_sem)
    local.start()
    sends = []
    for k in range(1, n):
        copy = pltpu.make_async_remote_copy(
            src_ref=part(lax.rem(me + k, n)),
            dst_ref=out_ref.at[me],
            send_sem=send_sem.at[k],
            recv_sem=recv_sem.at[k],
            device_id={axis: lax.rem(me + k, n)},
            device_id_type=mesh_id,
        )
        copy.start()
        sends.append(copy)
    for k in range(1, n):
        source = lax.rem(me + n - k, n)
        arriving = pltpu.make_async_remote_copy(
            src_ref=part(me),
            dst_ref=out_ref.at[source],
            send_sem=send_sem.at[k],
            recv_sem=recv_sem.at[k],
            device_id={axis: source},
            device_id_type=mesh_id,
        )
        arriving.wait_recv()
    for copy in sends:
        copy.wait_send()
    local.wait()


def dma_exchange(x, axis, collective_id, scatter):
    n = lax.axis_size(axis)
    out_shape = x.shape if scatter else (n,) + x.shape
    return pl.pallas_call(
        functools.partial(exchange_kernel, axis, n, scatter),
        in_specs=[pl.BlockSpec(memory_space=pl.ANY)],
        out_specs=pl.BlockSpec(memory_space=pl.ANY),
        out_shape=jax.ShapeDtypeStruct(out_shape, x.dtype),
        scratch_shapes=[
            pltpu.SemaphoreType.DMA((n,)),
            pltpu.SemaphoreType.DMA((n,)),
            pltpu.SemaphoreType.DMA,
        ],
        compiler_params=pltpu.CompilerParams(collective_id=collective_id, has_side_effects=True),
    )(x)


def per_device(
    features,
    edge_dst,
    edge_src,
    edge_mask,
    gin_in,
    gin_out,
    w_query,
    w_key,
    w_value,
    w_attn_out,
    ffn_in,
    ffn_out,
):
    rows, cols = features.shape
    n_mp = lax.axis_size("mp")
    width = cols * n_mp
    share = rows // n_mp
    me = lax.axis_index("mp")
    heads = w_query.shape[1] // HEAD_DIM
    scale = 1.0 / math.sqrt(HEAD_DIM)

    feature_parts_t = dma_exchange(features.T, "mp", 0, False)

    def project(w):
        return jnp.einsum(
            "jcr,jcd->rd",
            feature_parts_t,
            w.reshape(n_mp, cols, w.shape[1]),
            preferred_element_type=jnp.float32,
        ).astype(jnp.bfloat16)

    projected = project(jnp.concatenate([w_query, w_key, w_value], axis=1))
    queries = projected[:, : HEAD_DIM * heads] * jnp.bfloat16(scale)
    kv_all = lax.all_gather(projected[:, HEAD_DIM * heads :], "blk", axis=0, tiled=True)

    pieces = (gin_in.T, ffn_in.T, gin_out, w_attn_out, ffn_out)
    packed_weights = jnp.concatenate(pieces, axis=0)
    n_blk = lax.axis_size("blk")
    piece_rows = packed_weights.shape[0] // n_blk
    piece = lax.dynamic_slice_in_dim(
        packed_weights, lax.axis_index("blk") * piece_rows, piece_rows, 0
    )
    piece_parts = lax.all_gather(piece, "mp", axis=0, tiled=False)
    kv_all, piece_parts, late_features = lax.optimization_barrier((kv_all, piece_parts, features))
    all_features = lax.all_gather(
        late_features.reshape(rows // BLOCK, BLOCK, cols), "blk", axis=0, tiled=True
    )
    weight_parts = lax.all_gather(piece_parts, "blk", axis=1, tiled=True)
    unpacked = []
    offset = 0
    for x in pieces:
        unpacked.append(weight_parts[:, offset : offset + x.shape[0], :])
        offset += x.shape[0]
    gin_in_t, ffn_in_t, gin_out_parts, attn_out_parts, ffn_out_parts = unpacked

    attended = flash_attention(queries, kv_all, 0, heads)

    gathered = neighbour_sum(features, edge_dst, edge_src, edge_mask, all_features)
    local_share = (features.astype(jnp.float32) + gathered * 0.25).astype(jnp.bfloat16)

    mixed_in = jnp.concatenate([local_share, attended], axis=1).reshape(n_mp, share, -1)
    received = lax.all_to_all(mixed_in, "mp", 0, 0, tiled=False)
    own_rows = (
        lax.dynamic_slice_in_dim(feature_parts_t, me * share, share, 2)
        .transpose(2, 0, 1)
        .reshape(share, width)
        .astype(jnp.float32)
    )

    local_hidden = jax.nn.relu(
        jnp.einsum(
            "jrc,pqjc->rpq",
            received[:, :, :cols],
            gin_in_t.reshape(n_mp, cols, n_mp, cols),
            preferred_element_type=jnp.float32,
        )
    ).astype(jnp.bfloat16)
    mixed = (
        own_rows
        + jnp.einsum("rjc,jce->re", local_hidden, gin_out_parts, preferred_element_type=jnp.float32)
        + jnp.einsum("jrd,jde->re", received[:, :, cols:], attn_out_parts, preferred_element_type=jnp.float32)
    )
    row_average = jnp.sum(mixed, axis=1, keepdims=True) / width
    square_row = jnp.sum(mixed * mixed, axis=1, keepdims=True) / width
    normed = (
        (mixed - row_average) * lax.rsqrt(square_row - row_average * row_average + 1e-05)
    ).astype(jnp.bfloat16)
    ffn_hidden = jax.nn.relu(
        jnp.einsum("rk,jck->rjc", normed, ffn_in_t, preferred_element_type=jnp.float32)
    ).astype(jnp.bfloat16)
    out_rows = (
        mixed
        + jnp.einsum("rjc,jce->re", ffn_hidden, ffn_out_parts, preferred_element_type=jnp.float32)
    ).astype(jnp.bfloat16)
    out_parts = out_rows.reshape(share, n_mp, cols).transpose(1, 0, 2)
    return lax.all_to_all(out_parts, "mp", 0, 0, tiled=False).reshape(rows, cols)


def solution(mesh):
    return jax.shard_map(
        per_device,
        mesh=mesh,
        in_specs=(
            P("blk", "mp"),
            P("blk"),
            P("blk"),
            P("blk", None, None),
            P(None, "mp"),
            P("mp", None),
            P(None, "mp"),
            P(None, "mp"),
            P(None, "mp"),
            P("mp", None),
            P(None, "mp"),
            P("mp", None),
        ),
        out_specs=P("blk", "mp"),
        check_vma=False,
    )
```

```python
import functools
import math

import jax
import jax.numpy as jnp
from jax import lax
from jax.experimental import pallas as pl
from jax.experimental.pallas import tpu as pltpu
from jax.sharding import PartitionSpec as P

HEAD_DIM = 64
BLOCK = 128
Q_TILE = 1024
K_TILE = 4096


def neighbour_sum(features, edge_dst, edge_src, edge_mask, all_features):
    rows, cols = features.shape
    local_blocks = rows // BLOCK
    count = all_features.shape[0]
    blocks = all_features
    pulled = jnp.take(blocks, jnp.clip(edge_src, 0, count - 1), axis=0)
    summand_terms = jnp.einsum(
        "ers,esf->erf",
        edge_mask.astype(jnp.bfloat16),
        pulled,
        preferred_element_type=jnp.float32,
    )
    target_nodes = (
        edge_dst[:, None] == jnp.arange(local_blocks, dtype=jnp.int32)[None, :]
    ).astype(jnp.float32)
    running_total = jnp.einsum(
        "cy,cla->yla", target_nodes, summand_terms, precision=lax.Precision.HIGHEST
    )
    return running_total.reshape(rows, cols)


def flash_kernel(dim, q_ref, kv_ref, o_ref, m_ref, l_ref, acc_ref):
    j = pl.program_id(1)

    @pl.when(j == 0)
    def _():
        m_ref[...] = jnp.full(m_ref.shape, -jnp.inf, jnp.float32)
        l_ref[...] = jnp.zeros(l_ref.shape, jnp.float32)
        acc_ref[...] = jnp.zeros(acc_ref.shape, jnp.float32)

    kv = kv_ref[...]
    s = lax.dot_general(
        q_ref[...], kv, (((1,), (1,)), ((), ())), preferred_element_type=jnp.float32
    )
    m_prev = m_ref[:, :1]
    m_new = jnp.maximum(m_prev, jnp.max(s, axis=1, keepdims=True))
    alpha = jnp.exp(m_prev - m_new)
    p = jnp.exp(s - m_new)
    l_ref[...] = jnp.broadcast_to(alpha * l_ref[:, :1] + jnp.sum(p, axis=1, keepdims=True), l_ref.shape)
    acc_ref[...] = alpha * acc_ref[...] + jnp.dot(
        p.astype(jnp.bfloat16), kv, preferred_element_type=jnp.float32
    )
    m_ref[...] = jnp.broadcast_to(m_new, m_ref.shape)

    @pl.when(j == pl.num_programs(1) - 1)
    def _():
        o_ref[...] = (acc_ref[:, dim : 2 * dim] / l_ref[:, :1]).astype(o_ref.dtype)


def flash_attention(q, packed_all, head, heads):
    rows, dim = q.shape
    keys_n = packed_all.shape[0]
    tq = min(Q_TILE, rows)
    tk = min(K_TILE, keys_n)
    grid = (rows // tq, keys_n // tk)
    assert heads == 1
    lanes = 2 * dim
    q_pad = jnp.concatenate([q, jnp.zeros((rows, lanes - dim), q.dtype)], axis=1)
    return pl.pallas_call(
        functools.partial(flash_kernel, dim),
        grid=grid,
        in_specs=[
            pl.BlockSpec((tq, lanes), lambda i, j: (i, 0)),
            pl.BlockSpec((tk, lanes), lambda i, j: (j, 0)),
        ],
        out_specs=pl.BlockSpec((tq, dim), lambda i, j: (i, 0)),
        out_shape=jax.ShapeDtypeStruct((rows, dim), jnp.bfloat16),
        scratch_shapes=[
            pltpu.VMEM((tq, 128), jnp.float32),
            pltpu.VMEM((tq, 128), jnp.float32),
            pltpu.VMEM((tq, lanes), jnp.float32),
        ],
        compiler_params=pltpu.CompilerParams(
            dimension_semantics=("arbitrary", "arbitrary")
        ),
        cost_estimate=pl.CostEstimate(
            flops=4 * rows * keys_n * lanes,
            transcendentals=rows * keys_n,
            bytes_accessed=rows * lanes * 2 + grid[0] * keys_n * lanes * 2 + rows * dim * 2,
        ),
    )(q_pad, packed_all)


def exchange_kernel(axis, n, scatter, x_ref, out_ref, send_sem, recv_sem, local_sem):
    me = lax.axis_index(axis)
    mesh_id = pl.DeviceIdType.MESH
    barrier = pltpu.get_barrier_semaphore()
    for k in range(1, n):
        pl.semaphore_signal(
            barrier, inc=1, device_id={axis: lax.rem(me + k, n)}, device_id_type=mesh_id
        )
    pl.semaphore_wait(barrier, n - 1)
    def part(device):
        return x_ref.at[device] if scatter else x_ref

    local = pltpu.make_async_copy(part(me), out_ref.at[me], local_sem)
    local.start()
    sends = []
    for k in range(1, n):
        copy = pltpu.make_async_remote_copy(
            src_ref=part(lax.rem(me + k, n)),
            dst_ref=out_ref.at[me],
            send_sem=send_sem.at[k],
            recv_sem=recv_sem.at[k],
            device_id={axis: lax.rem(me + k, n)},
            device_id_type=mesh_id,
        )
        copy.start()
        sends.append(copy)
    for k in range(1, n):
        source = lax.rem(me + n - k, n)
        arriving = pltpu.make_async_remote_copy(
            src_ref=part(me),
            dst_ref=out_ref.at[source],
            send_sem=send_sem.at[k],
            recv_sem=recv_sem.at[k],
            device_id={axis: source},
            device_id_type=mesh_id,
        )
        arriving.wait_recv()
    for copy in sends:
        copy.wait_send()
    local.wait()


def dma_exchange(x, axis, collective_id, scatter):
    n = lax.axis_size(axis)
    out_shape = x.shape if scatter else (n,) + x.shape
    return pl.pallas_call(
        functools.partial(exchange_kernel, axis, n, scatter),
        in_specs=[pl.BlockSpec(memory_space=pl.ANY)],
        out_specs=pl.BlockSpec(memory_space=pl.ANY),
        out_shape=jax.ShapeDtypeStruct(out_shape, x.dtype),
        scratch_shapes=[
            pltpu.SemaphoreType.DMA((n,)),
            pltpu.SemaphoreType.DMA((n,)),
            pltpu.SemaphoreType.DMA,
        ],
        compiler_params=pltpu.CompilerParams(collective_id=collective_id, has_side_effects=True),
    )(x)


def per_device(
    features,
    edge_dst,
    edge_src,
    edge_mask,
    gin_in,
    gin_out,
    w_query,
    w_key,
    w_value,
    w_attn_out,
    ffn_in,
    ffn_out,
):
    rows, cols = features.shape
    n_mp = lax.axis_size("mp")
    width = cols * n_mp
    share = rows // n_mp
    me = lax.axis_index("mp")
    heads = w_query.shape[1] // HEAD_DIM
    scale = 1.0 / math.sqrt(HEAD_DIM)

    feature_parts_t = dma_exchange(features.T, "mp", 0, False)

    def project(w):
        return jnp.einsum(
            "jcr,jcd->rd",
            feature_parts_t,
            w.reshape(n_mp, cols, w.shape[1]),
            preferred_element_type=jnp.float32,
        ).astype(jnp.bfloat16)

    projected = project(jnp.concatenate([w_query, w_key, w_value], axis=1))
    queries = projected[:, : HEAD_DIM * heads] * jnp.bfloat16(scale)
    kv_all = lax.all_gather(projected[:, HEAD_DIM * heads :], "blk", axis=0, tiled=True)

    pieces = (gin_in.T, ffn_in.T, gin_out, w_attn_out, ffn_out)
    packed_weights = jnp.concatenate(pieces, axis=0)
    n_blk = lax.axis_size("blk")
    piece_rows = packed_weights.shape[0] // n_blk
    piece = lax.dynamic_slice_in_dim(
        packed_weights, lax.axis_index("blk") * piece_rows, piece_rows, 0
    )
    piece_parts = lax.all_gather(piece, "mp", axis=0, tiled=False)
    kv_all, piece_parts, late_features = lax.optimization_barrier((kv_all, piece_parts, features))
    all_features = lax.all_gather(
        late_features.reshape(rows // BLOCK, BLOCK, cols), "blk", axis=0, tiled=True
    )
    weight_parts = lax.all_gather(piece_parts, "blk", axis=1, tiled=True)
    unpacked = []
    offset = 0
    for x in pieces:
        unpacked.append(weight_parts[:, offset : offset + x.shape[0], :])
        offset += x.shape[0]
    gin_in_t, ffn_in_t, gin_out_parts, attn_out_parts, ffn_out_parts = unpacked

    attended = flash_attention(queries, kv_all, 0, heads)

    gathered = neighbour_sum(features, edge_dst, edge_src, edge_mask, all_features)
    local_share = (features.astype(jnp.float32) + gathered * 0.25).astype(jnp.bfloat16)

    mixed_in = (
        jnp.concatenate([local_share, attended], axis=1)
        .T.reshape(-1, n_mp, share)
        .transpose(1, 0, 2)
    )
    received = lax.all_to_all(mixed_in, "mp", 0, 0, tiled=False)
    own_rows = (
        lax.dynamic_slice_in_dim(feature_parts_t, me * share, share, 2)
        .transpose(2, 0, 1)
        .reshape(share, width)
        .astype(jnp.float32)
    )

    local_hidden = jax.nn.relu(
        jnp.einsum(
            "jcr,pqjc->rpq",
            received[:, :cols, :],
            gin_in_t.reshape(n_mp, cols, n_mp, cols),
            preferred_element_type=jnp.float32,
        )
    ).astype(jnp.bfloat16)
    mixed = (
        own_rows
        + jnp.einsum("rjc,jce->re", local_hidden, gin_out_parts, preferred_element_type=jnp.float32)
        + jnp.einsum("jdr,jde->re", received[:, cols:, :], attn_out_parts, preferred_element_type=jnp.float32)
    )
    row_average = jnp.sum(mixed, axis=1, keepdims=True) / width
    square_row = jnp.sum(mixed * mixed, axis=1, keepdims=True) / width
    normed = (
        (mixed - row_average) * lax.rsqrt(square_row - row_average * row_average + 1e-05)
    ).astype(jnp.bfloat16)
    ffn_hidden = jax.nn.relu(
        jnp.einsum("rk,jck->rjc", normed, ffn_in_t, preferred_element_type=jnp.float32)
    ).astype(jnp.bfloat16)
    out_rows = (
        mixed
        + jnp.einsum("rjc,jce->re", ffn_hidden, ffn_out_parts, preferred_element_type=jnp.float32)
    ).astype(jnp.bfloat16)
    out_parts = out_rows.reshape(share, n_mp, cols).transpose(1, 0, 2)
    return lax.all_to_all(out_parts, "mp", 0, 0, tiled=False).reshape(rows, cols)


def solution(mesh):
    return jax.shard_map(
        per_device,
        mesh=mesh,
        in_specs=(
            P("blk", "mp"),
            P("blk"),
            P("blk"),
            P("blk", None, None),
            P(None, "mp"),
            P("mp", None),
            P(None, "mp"),
            P(None, "mp"),
            P(None, "mp"),
            P("mp", None),
            P(None, "mp"),
            P("mp", None),
        ),
        out_specs=P("blk", "mp"),
        check_vma=False,
    )
```

```python
import functools
import math

import jax
import jax.numpy as jnp
from jax import lax
from jax.experimental import pallas as pl
from jax.experimental.pallas import tpu as pltpu
from jax.sharding import PartitionSpec as P

HEAD_DIM = 64
BLOCK = 128
Q_TILE = 1024
K_TILE = 4096


def neighbour_sum(features, edge_dst, edge_src, edge_mask, all_features):
    rows, cols = features.shape
    local_blocks = rows // BLOCK
    count = all_features.shape[0]
    blocks = all_features
    pulled = jnp.take(blocks, jnp.clip(edge_src, 0, count - 1), axis=0)
    summand_terms = jnp.einsum(
        "ers,esf->erf",
        edge_mask.astype(jnp.bfloat16),
        pulled,
        preferred_element_type=jnp.float32,
    )
    target_nodes = (
        edge_dst[:, None] == jnp.arange(local_blocks, dtype=jnp.int32)[None, :]
    ).astype(jnp.float32)
    running_total = jnp.einsum(
        "cy,cla->yla", target_nodes, summand_terms, precision=lax.Precision.HIGHEST
    )
    return running_total.reshape(rows, cols)


def flash_kernel(dim, q_ref, kv_ref, o_ref, m_ref, l_ref, acc_ref):
    j = pl.program_id(1)

    @pl.when(j == 0)
    def _():
        m_ref[...] = jnp.full(m_ref.shape, -jnp.inf, jnp.float32)
        l_ref[...] = jnp.zeros(l_ref.shape, jnp.float32)
        acc_ref[...] = jnp.zeros(acc_ref.shape, jnp.float32)

    kv = kv_ref[...]
    s = lax.dot_general(
        q_ref[...], kv, (((1,), (1,)), ((), ())), preferred_element_type=jnp.float32
    )
    m_prev = m_ref[:, :1]
    m_new = jnp.maximum(m_prev, jnp.max(s, axis=1, keepdims=True))
    alpha = jnp.exp(m_prev - m_new)
    p = jnp.exp(s - m_new)
    l_ref[...] = jnp.broadcast_to(alpha * l_ref[:, :1] + jnp.sum(p, axis=1, keepdims=True), l_ref.shape)
    acc_ref[...] = alpha * acc_ref[...] + jnp.dot(
        p.astype(jnp.bfloat16), kv, preferred_element_type=jnp.float32
    )
    m_ref[...] = jnp.broadcast_to(m_new, m_ref.shape)

    @pl.when(j == pl.num_programs(1) - 1)
    def _():
        o_ref[...] = (acc_ref[:, dim : 2 * dim] / l_ref[:, :1]).astype(o_ref.dtype)


def flash_attention(q, packed_all, head, heads):
    rows, dim = q.shape
    keys_n = packed_all.shape[0]
    tq = min(Q_TILE, rows)
    tk = min(K_TILE, keys_n)
    grid = (rows // tq, keys_n // tk)
    assert heads == 1
    lanes = 2 * dim
    q_pad = jnp.concatenate([q, jnp.zeros((rows, lanes - dim), q.dtype)], axis=1)
    return pl.pallas_call(
        functools.partial(flash_kernel, dim),
        grid=grid,
        in_specs=[
            pl.BlockSpec((tq, lanes), lambda i, j: (i, 0)),
            pl.BlockSpec((tk, lanes), lambda i, j: (j, 0)),
        ],
        out_specs=pl.BlockSpec((tq, dim), lambda i, j: (i, 0)),
        out_shape=jax.ShapeDtypeStruct((rows, dim), jnp.bfloat16),
        scratch_shapes=[
            pltpu.VMEM((tq, 128), jnp.float32),
            pltpu.VMEM((tq, 128), jnp.float32),
            pltpu.VMEM((tq, lanes), jnp.float32),
        ],
        compiler_params=pltpu.CompilerParams(
            dimension_semantics=("arbitrary", "arbitrary")
        ),
        cost_estimate=pl.CostEstimate(
            flops=4 * rows * keys_n * lanes,
            transcendentals=rows * keys_n,
            bytes_accessed=rows * lanes * 2 + grid[0] * keys_n * lanes * 2 + rows * dim * 2,
        ),
    )(q_pad, packed_all)


def exchange_kernel(axis, n, scatter, x_ref, out_ref, send_sem, recv_sem, local_sem):
    me = lax.axis_index(axis)
    mesh_id = pl.DeviceIdType.MESH
    barrier = pltpu.get_barrier_semaphore()
    for k in range(1, n):
        pl.semaphore_signal(
            barrier, inc=1, device_id={axis: lax.rem(me + k, n)}, device_id_type=mesh_id
        )
    pl.semaphore_wait(barrier, n - 1)
    def part(device):
        return x_ref.at[device] if scatter else x_ref

    local = pltpu.make_async_copy(part(me), out_ref.at[me], local_sem)
    local.start()
    sends = []
    for k in range(1, n):
        copy = pltpu.make_async_remote_copy(
            src_ref=part(lax.rem(me + k, n)),
            dst_ref=out_ref.at[me],
            send_sem=send_sem.at[k],
            recv_sem=recv_sem.at[k],
            device_id={axis: lax.rem(me + k, n)},
            device_id_type=mesh_id,
        )
        copy.start()
        sends.append(copy)
    for k in range(1, n):
        source = lax.rem(me + n - k, n)
        arriving = pltpu.make_async_remote_copy(
            src_ref=part(me),
            dst_ref=out_ref.at[source],
            send_sem=send_sem.at[k],
            recv_sem=recv_sem.at[k],
            device_id={axis: source},
            device_id_type=mesh_id,
        )
        arriving.wait_recv()
    for copy in sends:
        copy.wait_send()
    local.wait()


def dma_exchange(x, axis, collective_id, scatter):
    n = lax.axis_size(axis)
    out_shape = x.shape if scatter else (n,) + x.shape
    return pl.pallas_call(
        functools.partial(exchange_kernel, axis, n, scatter),
        in_specs=[pl.BlockSpec(memory_space=pl.ANY)],
        out_specs=pl.BlockSpec(memory_space=pl.ANY),
        out_shape=jax.ShapeDtypeStruct(out_shape, x.dtype),
        scratch_shapes=[
            pltpu.SemaphoreType.DMA((n,)),
            pltpu.SemaphoreType.DMA((n,)),
            pltpu.SemaphoreType.DMA,
        ],
        compiler_params=pltpu.CompilerParams(collective_id=collective_id, has_side_effects=True),
    )(x)


def per_device(
    features,
    edge_dst,
    edge_src,
    edge_mask,
    gin_in,
    gin_out,
    w_query,
    w_key,
    w_value,
    w_attn_out,
    ffn_in,
    ffn_out,
):
    rows, cols = features.shape
    n_mp = lax.axis_size("mp")
    width = cols * n_mp
    share = rows // n_mp
    me = lax.axis_index("mp")
    heads = w_query.shape[1] // HEAD_DIM
    scale = 1.0 / math.sqrt(HEAD_DIM)

    feature_parts_t = dma_exchange(features.T, "mp", 0, False)

    def project(w):
        return jnp.einsum(
            "jcr,jcd->rd",
            feature_parts_t,
            w.reshape(n_mp, cols, w.shape[1]),
            preferred_element_type=jnp.float32,
        ).astype(jnp.bfloat16)

    projected = project(jnp.concatenate([w_query, w_key, w_value], axis=1))
    queries = projected[:, : HEAD_DIM * heads] * jnp.bfloat16(scale)
    kv_all = lax.all_gather(projected[:, HEAD_DIM * heads :], "blk", axis=0, tiled=True)

    pieces = (gin_in.T, ffn_in.T, gin_out, w_attn_out, ffn_out)
    packed_weights = jnp.concatenate(pieces, axis=0)
    n_blk = lax.axis_size("blk")
    piece_rows = packed_weights.shape[0] // n_blk
    piece = lax.dynamic_slice_in_dim(
        packed_weights, lax.axis_index("blk") * piece_rows, piece_rows, 0
    )
    piece_parts = lax.all_gather(piece, "mp", axis=0, tiled=False)
    kv_all, piece_parts, late_features = lax.optimization_barrier((kv_all, piece_parts, features))
    all_features = lax.all_gather(
        late_features.reshape(rows // BLOCK, BLOCK, cols), "blk", axis=0, tiled=True
    )
    weight_parts = lax.all_gather(piece_parts, "blk", axis=1, tiled=True)
    unpacked = []
    offset = 0
    for x in pieces:
        unpacked.append(weight_parts[:, offset : offset + x.shape[0], :])
        offset += x.shape[0]
    gin_in_t, ffn_in_t, gin_out_parts, attn_out_parts, ffn_out_parts = unpacked

    attended = flash_attention(queries, kv_all, 0, heads)

    gathered = neighbour_sum(features, edge_dst, edge_src, edge_mask, all_features)
    local_share = (features.astype(jnp.float32) + gathered * 0.25).astype(jnp.bfloat16)

    mixed_in = (
        jnp.concatenate([local_share, attended], axis=1)
        .T.reshape(-1, n_mp, share)
        .transpose(1, 0, 2)
    )
    received = lax.all_to_all(mixed_in, "mp", 0, 0, tiled=False)
    own_rows = (
        lax.dynamic_slice_in_dim(feature_parts_t, me * share, share, 2)
        .transpose(2, 0, 1)
        .reshape(share, width)
        .astype(jnp.float32)
    )

    local_hidden = jax.nn.relu(
        jnp.einsum(
            "jcr,pqjc->rpq",
            received[:, :cols, :],
            gin_in_t.reshape(n_mp, cols, n_mp, cols),
            preferred_element_type=jnp.float32,
        )
    ).astype(jnp.bfloat16)
    mixed = (
        own_rows
        + jnp.einsum("rjc,jce->re", local_hidden, gin_out_parts, preferred_element_type=jnp.float32)
        + jnp.einsum("jdr,jde->re", received[:, cols:, :], attn_out_parts, preferred_element_type=jnp.float32)
    )
    row_average = jnp.sum(mixed, axis=1, keepdims=True) / width
    square_row = jnp.sum(mixed * mixed, axis=1, keepdims=True) / width
    normed = (
        (mixed - row_average) * lax.rsqrt(square_row - row_average * row_average + 1e-05)
    ).astype(jnp.bfloat16)
    ffn_hidden = jax.nn.relu(
        jnp.einsum("rk,jck->rjc", normed, ffn_in_t, preferred_element_type=jnp.float32)
    ).astype(jnp.bfloat16)
    out_rows = (
        mixed
        + jnp.einsum("rjc,jce->re", ffn_hidden, ffn_out_parts, preferred_element_type=jnp.float32)
    ).astype(jnp.bfloat16)
    out_parts = out_rows.T.reshape(n_mp, cols, share)
    received_out = lax.all_to_all(out_parts, "mp", 0, 0, tiled=False)
    return received_out.transpose(1, 0, 2).reshape(cols, rows).T


def solution(mesh):
    return jax.shard_map(
        per_device,
        mesh=mesh,
        in_specs=(
            P("blk", "mp"),
            P("blk"),
            P("blk"),
            P("blk", None, None),
            P(None, "mp"),
            P("mp", None),
            P(None, "mp"),
            P(None, "mp"),
            P(None, "mp"),
            P("mp", None),
            P(None, "mp"),
            P("mp", None),
        ),
        out_specs=P("blk", "mp"),
        check_vma=False,
    )
```
